32 devices in a mesh: col: 4 (over z), row: 8 (over y, x, core).
Axes of the slice: x: 2, y: 2, z: 4, core: 2. Of those that a mesh axis runs over, the one named last changes fastest.
Arguments:
- sources: bfloat16 [131072, 1024], P(('col', 'row')), may hold values from -6 to 6
- enc_scale: float32 [131072], P(('col', 'row')), may hold values from 0.5 to 2
- encoder: bfloat16 [256, 4096], replicated, may hold values from -0.09375 to 0.09375
- comp_transfer: bfloat16 [2, 512, 512], replicated, may hold values from -0.25 to 0.25
- comp_gain: float32 [2, 8, 4, 256], P(None, 'row'), may hold values from 0.5 to 1.5
- exp_transfer: bfloat16 [3, 512, 512], replicated, may hold values from -0.25 to 0.25
- exp_gain: float32 [3, 4, 8, 256], P(None, 'col'), may hold values from 0.5 to 1.5
- decoder: bfloat16 [4096, 256], replicated, may hold values from -0.375 to 0.375
- dec_scale: float32 [131072], P(('col', 'row')), may hold values from 0.5 to 2
Outputs:
- field: bfloat16 [131072, 1024], P(('col', 'row'))
The draws below stay inside these ranges and needn't reach their ends.
All inputs are finite; a program needn't handle non-finite values.
Results may differ from the reference program's by a relative error of at most 0.015.
Values may be sent and summed in bfloat16 or wider, within the bound.
No kernel may reach another device: no remote copies, remote signals or barrier semaphores. Data moves between devices by JAX's collectives and lax.ppermute only.
A program may use at most 128 MiB of HBM per device.

```python
import math
import jax
import jax.numpy as jnp
from jax import lax

LEAF = 4096
SKEL = 256
SOURCES = 1024
CGROUPS = 4
RGROUPS = 8
UNKNOWNS = 131072
CLEVELS = 2
RLEVELS = 3
N_COL = 4
N_ROW = 8


def level_of(key, shape, pieces, smallest, top_value):
    level, own = 1.0, jax.random.fold_in(key, 6)
    for position, shards_of in pieces:
        draws = jnp.exp(jax.random.uniform(jax.random.fold_in(own, position), (shards_of,), jnp.float32, smallest / len(pieces), top_value / len(pieces)))
        level = level * jnp.repeat(draws, shape[position] // shards_of).reshape([-1 if axis == position else 1 for axis in range(len(shape))])
    return level


def noise(key, shape, width, reach, cuts=(), dtype=jnp.bfloat16):
    values = width * jax.random.normal(key, shape, jnp.float32)
    if cuts:
        values = values * level_of(key, shape, cuts, -0.22, 0.18)
    return jnp.clip(values, -reach, reach).astype(dtype)


def setup_inputs(seed: int = 0) -> dict:
    arg_keys = jax.random.split(jax.random.key(seed), 10)
    return {
        "sources": noise(arg_keys[0], (UNKNOWNS, SOURCES), 1.0, 6.0, ((0, 32),)),
        "enc_scale": jnp.clip(jnp.exp(math.log(2.0) - 1.3862944 * jax.random.uniform(arg_keys[1], (UNKNOWNS,), jnp.float32) ** level_of(arg_keys[1], (UNKNOWNS,), ((0, 32),), -0.2, 0.2)), 0.5, 2.0),
        "encoder": noise(arg_keys[2], (SKEL, LEAF), LEAF ** -0.5, 0.09375),
        "comp_transfer": noise(arg_keys[3], (CLEVELS, 2 * SKEL, 2 * SKEL), (2 * SKEL) ** -0.5, 0.25),
        "comp_gain": jnp.clip(jnp.exp(math.log(1.5) - 1.0986123 * jax.random.uniform(arg_keys[4], (CLEVELS, RGROUPS, CGROUPS, SKEL), jnp.float32) ** level_of(arg_keys[4], (CLEVELS, RGROUPS, CGROUPS, SKEL), ((1, 8),), -0.2, 0.2)), 0.5, 1.5),
        "exp_transfer": noise(arg_keys[5], (RLEVELS, 2 * SKEL, 2 * SKEL), (2 * SKEL) ** -0.5, 0.25),
        "exp_gain": jnp.clip(jnp.exp(math.log(1.5) - 1.0986123 * jax.random.uniform(arg_keys[6], (RLEVELS, CGROUPS, RGROUPS, SKEL), jnp.float32) ** level_of(arg_keys[6], (RLEVELS, CGROUPS, RGROUPS, SKEL), ((1, 4),), -0.2, 0.2)), 0.5, 1.5),
        "decoder": noise(arg_keys[7], (LEAF, SKEL), SKEL ** -0.5, 0.375),
        "dec_scale": jnp.clip(jnp.exp(math.log(2.0) - 1.3862944 * jax.random.uniform(arg_keys[8], (UNKNOWNS,), jnp.float32) ** level_of(arg_keys[8], (UNKNOWNS,), ((0, 32),), -0.2, 0.2)), 0.5, 2.0),
    }


def reference(sources, enc_scale, encoder, comp_transfer, comp_gain, exp_transfer, exp_gain, decoder, dec_scale):
    leaves = N_COL * N_ROW
    leaf_data = sources.reshape(leaves, LEAF, SOURCES)
    leaf_scale = enc_scale.reshape(leaves, LEAF, 1)

    def encode(packed):
        leaf_block, weight = packed
        scaled = (leaf_block.astype(jnp.float32) * weight).astype(jnp.bfloat16)
        return jnp.dot(scaled.T, encoder.T, preferred_element_type=jnp.float32).astype(jnp.bfloat16)

    coeffs = lax.map(encode, (leaf_data, leaf_scale)).reshape(N_COL, N_ROW, SOURCES, SKEL)
    for level_num in range(CLEVELS):
        lower_span = 2 ** level_num
        upper_span = N_COL // (2 * lower_span)
        halves = coeffs.reshape(upper_span, 2, lower_span, N_ROW, SOURCES, SKEL)
        stacked = jnp.concatenate([halves[:, 0], halves[:, 1]], axis=-1).astype(jnp.float32)
        transfer = comp_transfer[level_num].astype(jnp.float32).reshape(2, SKEL, 2 * SKEL)
        mixed_rows = jnp.einsum('hlqsk,tjk->htlqsj', stacked, transfer)
        mixed_rows = mixed_rows.reshape(N_COL, N_ROW, SOURCES, SKEL)
        gain_table = jnp.transpose(comp_gain[level_num], (1, 0, 2))[:, :, None, :]
        coeffs = (mixed_rows * gain_table).astype(jnp.bfloat16)
    for level_num in range(RLEVELS):
        lower_span = 2 ** level_num
        upper_span = N_ROW // (2 * lower_span)
        halves = coeffs.reshape(N_COL, upper_span, 2, lower_span, SOURCES, SKEL)
        stacked = jnp.concatenate([halves[:, :, 0], halves[:, :, 1]], axis=-1).astype(jnp.float32)
        transfer = exp_transfer[level_num].astype(jnp.float32).reshape(2, SKEL, 2 * SKEL)
        mixed_rows = jnp.einsum('chlsk,tjk->chtlsj', stacked, transfer)
        mixed_rows = mixed_rows.reshape(N_COL, N_ROW, SOURCES, SKEL)
        gain_table = exp_gain[level_num][:, :, None, :]
        coeffs = (mixed_rows * gain_table).astype(jnp.bfloat16)
    blocks = coeffs.reshape(leaves, SOURCES, SKEL)
    out_scale = dec_scale.reshape(leaves, LEAF, 1)

    def decode(packed):
        leaf_block, weight = packed
        result = jnp.dot(decoder, leaf_block.T, preferred_element_type=jnp.float32)
        return (result * weight).astype(jnp.bfloat16)

    return lax.map(decode, (blocks, out_scale)).reshape(LEAF * leaves, SOURCES)
```

```python
import functools

import jax
import jax.numpy as jnp
from jax import lax
from jax.experimental import pallas as pl
from jax.experimental.pallas import tpu as pltpu
from jax.sharding import PartitionSpec as P

AXES = ("col", "row")
LANES = 128
NT = (((1,), (1,)), ((), ()))


def mm(a, b, dims=(((1,), (0,)), ((), ()))):
    return lax.dot_general(a, b, dims, preferred_element_type=jnp.float32)


def encode_kernel(sources_ref, scale_ref, encoder_ref, gains_ref, out_ref, acc_ref):
    step = pl.program_id(0)
    scaled = (encoder_ref[...].astype(jnp.float32) * scale_ref[...]).astype(jnp.bfloat16)
    part = mm(scaled, sources_ref[...])

    @pl.when(step == 0)
    def _():
        acc_ref[...] = part

    @pl.when(step > 0)
    def _():
        acc_ref[...] += part

    @pl.when(step == pl.num_programs(0) - 1)
    def _():
        parts = out_ref.shape[0]
        pad = gains_ref.shape[0]
        width = (out_ref.shape[1] - pad) // 2
        turned = acc_ref[...].T.astype(jnp.bfloat16).reshape(parts, width, 2 * LANES)
        out_ref[:, :width, :] = turned[:, :, :LANES]
        out_ref[:, width : 2 * width, :] = turned[:, :, LANES:]
        out_ref[:, 2 * width :, :] = jnp.broadcast_to(gains_ref[...][None], (parts, pad, LANES))


def encode(sources, enc_scale, encoder, gains, parts):
    points, width = sources.shape
    skeleton = encoder.shape[0]
    pad = gains.shape[0]
    block = 512
    rows = 2 * (width // parts) + pad
    return pl.pallas_call(
        encode_kernel,
        grid=(points // block,),
        in_specs=[
            pl.BlockSpec((block, width), lambda k: (k, 0)),
            pl.BlockSpec((1, block), lambda k: (0, k)),
            pl.BlockSpec((skeleton, block), lambda k: (0, k)),
            pl.BlockSpec((pad, LANES), lambda k: (0, 0)),
        ],
        out_specs=pl.BlockSpec((parts, rows, LANES), lambda k: (0, 0, 0)),
        out_shape=jax.ShapeDtypeStruct((parts, rows, LANES), jnp.bfloat16),
        scratch_shapes=[pltpu.VMEM((skeleton, width), jnp.float32)],
        compiler_params=pltpu.CompilerParams(dimension_semantics=("arbitrary",)),
    )(sources, enc_scale.reshape(1, points), encoder, gains)


def levels_kernel(strides, pad, packed_ref, comp_ref, exp_ref, out_ref):
    boxes, rows, _ = packed_ref.shape
    width = (rows - pad) // 2
    skeleton = 2 * LANES
    state = jnp.concatenate([packed_ref[:, :width, :], packed_ref[:, width : 2 * width, :]], axis=-1)
    gains = packed_ref[:, 2 * width :, :].astype(jnp.float32)
    for number, stride in enumerate(strides):
        turned = number >= comp_ref.shape[0]
        transfer = exp_ref[number - comp_ref.shape[0]] if turned else comp_ref[number]
        halves = state.reshape(boxes // (2 * stride), 2, stride * width, skeleton)
        low = halves[:, 0].reshape(boxes // 2 * width, skeleton)
        high = halves[:, 1].reshape(boxes // 2 * width, skeleton)
        mixed = mm(low, transfer[:, :skeleton], NT) + mm(high, transfer[:, skeleton:], NT)
        shape = (boxes // (2 * stride), 1, stride, width, skeleton)
        both = jnp.concatenate(
            [mixed[:, :skeleton].reshape(shape), mixed[:, skeleton:].reshape(shape)], axis=1
        ).reshape(boxes, width, skeleton)
        if number + 1 < len(strides):
            gain = jnp.concatenate(
                [gains[:, 2 * number : 2 * number + 1, :], gains[:, 2 * number + 1 : 2 * number + 2, :]],
                axis=-1,
            )
            both = both * gain
        state = both.astype(jnp.bfloat16)
    out_ref[:, :width, :] = state[:, :, :LANES]
    out_ref[:, width:, :] = state[:, :, LANES:]


def levels(packed, comp_transfer, exp_transfer, strides, pad):
    boxes, rows, _ = packed.shape
    return pl.pallas_call(
        functools.partial(levels_kernel, strides, pad),
        in_specs=[pl.BlockSpec(memory_space=pltpu.VMEM)] * 3,
        out_specs=pl.BlockSpec(memory_space=pltpu.VMEM),
        out_shape=jax.ShapeDtypeStruct((boxes, rows - pad, LANES), jnp.bfloat16),
    )(packed, comp_transfer, exp_transfer)


def decode_kernel(packed_ref, decoder_ref, out_ref, turned_ref):
    @pl.when(pl.program_id(0) == 0)
    def _():
        boxes, rows, _ = packed_ref.shape
        width = rows // 2
        coeffs = jnp.concatenate([packed_ref[:, :width, :], packed_ref[:, width:, :]], axis=-1)
        turned_ref[...] = coeffs.reshape(boxes * width, 2 * LANES).T

    out_ref[...] = mm(decoder_ref[...], turned_ref[...]).astype(jnp.bfloat16)


def decode(packed, decoder):
    boxes, rows, _ = packed.shape
    points, skeleton = decoder.shape
    width = boxes * rows // 2
    block = 512
    return pl.pallas_call(
        decode_kernel,
        grid=(points // block,),
        in_specs=[
            pl.BlockSpec((boxes, rows, LANES), lambda k: (0, 0, 0)),
            pl.BlockSpec((block, skeleton), lambda k: (k, 0)),
        ],
        out_specs=pl.BlockSpec((block, width), lambda k: (k, 0)),
        out_shape=jax.ShapeDtypeStruct((points, width), jnp.bfloat16),
        scratch_shapes=[pltpu.VMEM((skeleton, width), jnp.bfloat16)],
        compiler_params=pltpu.CompilerParams(dimension_semantics=("arbitrary",)),
    )(packed, decoder)


def plain_encode(sources, enc_scale, encoder, gains, parts):
    scaled = (encoder.astype(jnp.float32) * enc_scale[None, :]).astype(jnp.bfloat16)
    coeffs = mm(sources, scaled, (((0,), (1,)), ((), ()))).astype(jnp.bfloat16)
    coeffs = coeffs.reshape(parts, -1, 2, LANES).swapaxes(1, 2).reshape(parts, -1, LANES)
    gains = jnp.broadcast_to(gains[None], (parts, *gains.shape))
    return jnp.concatenate([coeffs, gains], axis=1)


def plain_levels(packed, comp_transfer, exp_transfer, strides, pad):
    boxes, rows, _ = packed.shape
    width = (rows - pad) // 2
    skeleton = 2 * LANES
    state = packed[:, : 2 * width].reshape(boxes, 2, width, LANES).swapaxes(1, 2).reshape(boxes, width, skeleton)
    gains = packed[:, 2 * width :].astype(jnp.float32).reshape(boxes, pad // 2, 1, skeleton)
    transfers = jnp.concatenate([comp_transfer, exp_transfer], axis=0)
    for number, stride in enumerate(strides):
        halves = state.reshape(boxes // (2 * stride), 2, stride, width, skeleton)
        stacked = jnp.concatenate([halves[:, 0], halves[:, 1]], axis=-1)
        paired = transfers[number].reshape(2, skeleton, 2 * skeleton)
        both = jnp.einsum("hlsk,tjk->htlsj", stacked, paired, preferred_element_type=jnp.float32)
        both = both.reshape(boxes, width, skeleton)
        if number + 1 < len(strides):
            both = both * gains[:, number]
        state = both.astype(jnp.bfloat16)
    return state.reshape(boxes, width, 2, LANES).swapaxes(1, 2).reshape(boxes, 2 * width, LANES)


def plain_decode(packed, decoder):
    boxes, rows, _ = packed.shape
    width = rows // 2
    coeffs = packed.reshape(boxes, 2, width, LANES).swapaxes(1, 2).reshape(boxes * width, 2 * LANES)
    return mm(decoder, coeffs, NT).astype(jnp.bfloat16)


def body(
    sources,
    enc_scale,
    encoder,
    comp_transfer,
    comp_gain,
    exp_transfer,
    exp_gain,
    decoder,
    dec_scale,
):
    col_count, row_count = lax.axis_size("col"), lax.axis_size("row")
    parts = col_count * row_count
    skeleton = encoder.shape[0]
    comp_levels, exp_levels = comp_transfer.shape[0], exp_transfer.shape[0]
    strides = tuple(row_count * 2**number for number in range(comp_levels)) + tuple(
        2**number for number in range(exp_levels)
    )
    own_comp = lax.dynamic_index_in_dim(comp_gain[:, 0], lax.axis_index("col"), 1, keepdims=False)
    own_exp = lax.dynamic_index_in_dim(exp_gain[:, 0], lax.axis_index("row"), 1, keepdims=False)
    sent = jnp.concatenate([own_comp, own_exp[:-1]], axis=0).astype(jnp.bfloat16).reshape(-1, LANES)
    pad = -(-sent.shape[0] // 8) * 8
    sent = jnp.pad(sent, ((0, pad - sent.shape[0]), (0, 0)))

    kernels = (sources.shape[1] // parts) % 16 == 0 and skeleton == 2 * LANES
    run_encode, run_levels, run_decode = (
        (encode, levels, decode) if kernels else (plain_encode, plain_levels, plain_decode)
    )
    packed = run_encode(sources, enc_scale, encoder, sent, parts)
    packed = lax.all_to_all(packed, AXES, 0, 0, tiled=True)
    result = run_levels(packed, comp_transfer, exp_transfer, strides, pad)
    result = lax.all_to_all(result, AXES, 0, 0, tiled=True)
    factors = dec_scale[:, None] * own_exp[-1][None, :]
    scaled = (decoder.astype(jnp.float32) * factors).astype(jnp.bfloat16)
    return run_decode(result, scaled)


def solution(mesh):
    in_specs = (
        P(AXES, None),
        P(AXES),
        P(),
        P(),
        P(None, "row", None, None),
        P(),
        P(None, "col", None, None),
        P(),
        P(AXES),
    )
    return jax.shard_map(body, mesh=mesh, in_specs=in_specs, out_specs=P(AXES, None), check_vma=False)
```

```python
import functools

import jax
import jax.numpy as jnp
from jax import lax
from jax.experimental import pallas as pl
from jax.experimental.pallas import tpu as pltpu
from jax.sharding import PartitionSpec as P

AXES = ("col", "row")
LANES = 128
NT = (((1,), (1,)), ((), ()))
HBM = pl.BlockSpec(memory_space=pl.ANY)
VMEM = pl.BlockSpec(memory_space=pltpu.VMEM)


def on_chip(value):
    return pltpu.with_memory_space_constraint(value, pltpu.VMEM)


def mm(a, b, dims=(((1,), (0,)), ((), ()))):
    return lax.dot_general(a, b, dims, preferred_element_type=jnp.float32)


def encode_kernel(blocks, sources_hbm, scale_ref, encoder_hbm, comp_ref, exp_ref, out_ref, held, table, acc_ref, sems):
    block = sources_hbm.shape[0] // blocks
    copies = []
    for number in range(blocks):
        span = pl.ds(number * block, block)
        copies.append(
            (
                pltpu.make_async_copy(encoder_hbm.at[:, span], table.at[:, span], sems.at[0, number]),
                pltpu.make_async_copy(sources_hbm.at[span], held.at[span], sems.at[1, number]),
            )
        )
        for copy in copies[-1]:
            copy.start()

    parts, rows, _ = out_ref.shape
    own = [comp_ref[number, pl.ds(lax.axis_index("col"), 1), :] for number in range(comp_ref.shape[0])]
    own += [exp_ref[number, pl.ds(lax.axis_index("row"), 1), :] for number in range(exp_ref.shape[0] - 1)]
    gains = [half for gain in own for half in (gain[:, :LANES], gain[:, LANES:])]
    pad = -(-len(gains) // 8) * 8
    gains += [jnp.zeros((1, LANES), jnp.float32)] * (pad - len(gains))
    gains = jnp.concatenate(gains, axis=0).astype(jnp.bfloat16)
    width = (rows - pad) // 2

    for number in range(blocks):
        for copy in copies[number]:
            copy.wait()
        span = slice(number * block, (number + 1) * block)
        scaled = (table[:, span].astype(jnp.float32) * scale_ref[:, span]).astype(jnp.bfloat16)
        part = mm(scaled, held[span, :])
        if number == 0:
            acc_ref[...] = part
        else:
            acc_ref[...] += part

    turned = acc_ref[...].T.astype(jnp.bfloat16).reshape(parts, width, 2 * LANES)
    out_ref[:, :width, :] = turned[:, :, :LANES]
    out_ref[:, width : 2 * width, :] = turned[:, :, LANES:]
    out_ref[:, 2 * width :, :] = jnp.broadcast_to(gains[None], (parts, pad, LANES))


def encode(sources, enc_scale, encoder, comp_gain, exp_gain, parts):
    points, width = sources.shape
    skeleton = encoder.shape[0]
    pad = gain_rows(comp_gain, exp_gain)
    blocks = 8
    return pl.pallas_call(
        functools.partial(encode_kernel, blocks),
        in_specs=[HBM, VMEM, HBM, VMEM, VMEM],
        out_specs=VMEM,
        out_shape=jax.ShapeDtypeStruct((parts, 2 * (width // parts) + pad, LANES), jnp.bfloat16),
        scratch_shapes=[
            pltpu.VMEM((points, width), jnp.bfloat16),
            pltpu.VMEM((skeleton, points), jnp.bfloat16),
            pltpu.VMEM((skeleton, width), jnp.float32),
            pltpu.SemaphoreType.DMA((2, blocks)),
        ],
    )(sources, enc_scale.reshape(1, points), encoder, comp_gain, exp_gain)


def gain_rows(comp_gain, exp_gain):
    sent = 2 * (comp_gain.shape[0] + exp_gain.shape[0] - 1)
    return -(-sent // 8) * 8


def levels_kernel(strides, pad, packed_ref, comp_ref, exp_ref, out_ref):
    boxes, rows, _ = packed_ref.shape
    width = (rows - pad) // 2
    skeleton = 2 * LANES
    state = jnp.concatenate([packed_ref[:, :width, :], packed_ref[:, width : 2 * width, :]], axis=-1)
    gains = packed_ref[:, 2 * width :, :].astype(jnp.float32)
    for number, stride in enumerate(strides):
        turned = number >= comp_ref.shape[0]
        transfer = exp_ref[number - comp_ref.shape[0]] if turned else comp_ref[number]
        halves = state.reshape(boxes // (2 * stride), 2, stride * width, skeleton)
        low = halves[:, 0].reshape(boxes // 2 * width, skeleton)
        high = halves[:, 1].reshape(boxes // 2 * width, skeleton)
        mixed = mm(low, transfer[:, :skeleton], NT) + mm(high, transfer[:, skeleton:], NT)
        shape = (boxes // (2 * stride), 1, stride, width, skeleton)
        both = jnp.concatenate(
            [mixed[:, :skeleton].reshape(shape), mixed[:, skeleton:].reshape(shape)], axis=1
        ).reshape(boxes, width, skeleton)
        if number + 1 < len(strides):
            gain = jnp.concatenate(
                [gains[:, 2 * number : 2 * number + 1, :], gains[:, 2 * number + 1 : 2 * number + 2, :]],
                axis=-1,
            )
            both = both * gain
        state = both.astype(jnp.bfloat16)
    out_ref[:, :width, :] = state[:, :, :LANES]
    out_ref[:, width:, :] = state[:, :, LANES:]


def levels(packed, comp_transfer, exp_transfer, strides, pad):
    boxes, rows, _ = packed.shape
    return pl.pallas_call(
        functools.partial(levels_kernel, strides, pad),
        in_specs=[VMEM] * 3,
        out_specs=VMEM,
        out_shape=jax.ShapeDtypeStruct((boxes, rows - pad, LANES), jnp.bfloat16),
    )(on_chip(packed), on_chip(comp_transfer), on_chip(exp_transfer))


def decode_kernel(blocks, packed_ref, decoder_ref, out_hbm, turned_ref, held, sems):
    boxes, rows, _ = packed_ref.shape
    width = rows // 2
    block = decoder_ref.shape[0] // blocks
    coeffs = jnp.concatenate([packed_ref[:, :width, :], packed_ref[:, width:, :]], axis=-1)
    turned_ref[...] = coeffs.reshape(boxes * width, 2 * LANES).T
    copies = []
    for number in range(blocks):
        span = pl.ds(number * block, block)
        rows_of = slice(number * block, (number + 1) * block)
        held[rows_of, :] = mm(decoder_ref[rows_of, :], turned_ref[...]).astype(jnp.bfloat16)
        copies.append(pltpu.make_async_copy(held.at[span], out_hbm.at[span], sems.at[number]))
        copies[-1].start()
    for copy in copies:
        copy.wait()


def decode(packed, decoder):
    boxes, rows, _ = packed.shape
    points, skeleton = decoder.shape
    width = boxes * rows // 2
    blocks = 8
    return pl.pallas_call(
        functools.partial(decode_kernel, blocks),
        in_specs=[VMEM, VMEM],
        out_specs=HBM,
        out_shape=jax.ShapeDtypeStruct((points, width), jnp.bfloat16),
        scratch_shapes=[
            pltpu.VMEM((skeleton, width), jnp.bfloat16),
            pltpu.VMEM((points, width), jnp.bfloat16),
            pltpu.SemaphoreType.DMA((blocks,)),
        ],
    )(on_chip(packed), on_chip(decoder))


def plain_encode(sources, enc_scale, encoder, comp_gain, exp_gain, parts):
    own_comp = lax.dynamic_index_in_dim(comp_gain, lax.axis_index("col"), 1, keepdims=False)
    own_exp = lax.dynamic_index_in_dim(exp_gain, lax.axis_index("row"), 1, keepdims=False)
    gains = jnp.concatenate([own_comp, own_exp[:-1]], axis=0).astype(jnp.bfloat16).reshape(-1, LANES)
    gains = jnp.pad(gains, ((0, gain_rows(comp_gain, exp_gain) - gains.shape[0]), (0, 0)))
    scaled = (encoder.astype(jnp.float32) * enc_scale[None, :]).astype(jnp.bfloat16)
    coeffs = mm(sources, scaled, (((0,), (1,)), ((), ()))).astype(jnp.bfloat16)
    coeffs = coeffs.reshape(parts, -1, 2, LANES).swapaxes(1, 2).reshape(parts, -1, LANES)
    gains = jnp.broadcast_to(gains[None], (parts, *gains.shape))
    return jnp.concatenate([coeffs, gains], axis=1)


def plain_levels(packed, comp_transfer, exp_transfer, strides, pad):
    boxes, rows, _ = packed.shape
    width = (rows - pad) // 2
    skeleton = 2 * LANES
    state = packed[:, : 2 * width].reshape(boxes, 2, width, LANES).swapaxes(1, 2).reshape(boxes, width, skeleton)
    gains = packed[:, 2 * width :].astype(jnp.float32).reshape(boxes, pad // 2, 1, skeleton)
    transfers = jnp.concatenate([comp_transfer, exp_transfer], axis=0)
    for number, stride in enumerate(strides):
        halves = state.reshape(boxes // (2 * stride), 2, stride, width, skeleton)
        stacked = jnp.concatenate([halves[:, 0], halves[:, 1]], axis=-1)
        paired = transfers[number].reshape(2, skeleton, 2 * skeleton)
        both = jnp.einsum("hlsk,tjk->htlsj", stacked, paired, preferred_element_type=jnp.float32)
        both = both.reshape(boxes, width, skeleton)
        if number + 1 < len(strides):
            both = both * gains[:, number]
        state = both.astype(jnp.bfloat16)
    return state.reshape(boxes, width, 2, LANES).swapaxes(1, 2).reshape(boxes, 2 * width, LANES)


def plain_decode(packed, decoder):
    boxes, rows, _ = packed.shape
    width = rows // 2
    coeffs = packed.reshape(boxes, 2, width, LANES).swapaxes(1, 2).reshape(boxes * width, 2 * LANES)
    return mm(decoder, coeffs, NT).astype(jnp.bfloat16)


def body(
    sources,
    enc_scale,
    encoder,
    comp_transfer,
    comp_gain,
    exp_transfer,
    exp_gain,
    decoder,
    dec_scale,
):
    col_count, row_count = lax.axis_size("col"), lax.axis_size("row")
    parts = col_count * row_count
    skeleton = encoder.shape[0]
    comp_levels, exp_levels = comp_transfer.shape[0], exp_transfer.shape[0]
    strides = tuple(row_count * 2**number for number in range(comp_levels)) + tuple(
        2**number for number in range(exp_levels)
    )
    comp_gain, exp_gain = comp_gain[:, 0], exp_gain[:, 0]
    pad = gain_rows(comp_gain, exp_gain)
    last_gain = lax.dynamic_index_in_dim(exp_gain[-1], lax.axis_index("row"), 0, keepdims=False)

    kernels = (sources.shape[1] // parts) % 16 == 0 and skeleton == 2 * LANES
    run_encode, run_levels, run_decode = (
        (encode, levels, decode) if kernels else (plain_encode, plain_levels, plain_decode)
    )
    packed = run_encode(sources, enc_scale, encoder, comp_gain, exp_gain, parts)
    packed = lax.all_to_all(packed, AXES, 0, 0, tiled=True)
    result = run_levels(packed, comp_transfer, exp_transfer, strides, pad)
    result = lax.all_to_all(result, AXES, 0, 0, tiled=True)
    factors = dec_scale[:, None] * last_gain[None, :]
    scaled = (decoder.astype(jnp.float32) * factors).astype(jnp.bfloat16)
    return run_decode(result, scaled)


def solution(mesh):
    in_specs = (
        P(AXES, None),
        P(AXES),
        P(),
        P(),
        P(None, "row", None, None),
        P(),
        P(None, "col", None, None),
        P(),
        P(AXES),
    )
    return jax.shard_map(body, mesh=mesh, in_specs=in_specs, out_specs=P(AXES, None), check_vma=False)
```

```python
import functools

import jax
import jax.numpy as jnp
from jax import lax
from jax.experimental import pallas as pl
from jax.experimental.pallas import tpu as pltpu
from jax.sharding import PartitionSpec as P


AXES = ("col", "row")
LANES = 128
NT = (((1,), (1,)), ((), ()))
HBM = pl.BlockSpec(memory_space=pltpu.HBM)
VMEM = pl.BlockSpec(memory_space=pltpu.VMEM)


def on_chip(value):
    return pltpu.with_memory_space_constraint(value, pltpu.VMEM)


def in_hbm(value):
    return pltpu.with_memory_space_constraint(value, pltpu.HBM)


def mm(a, b, dims=(((1,), (0,)), ((), ()))):
    return lax.dot_general(a, b, dims, preferred_element_type=jnp.float32)


def start_loads(blocks, first, sources_hbm, encoder_hbm, held, table, sems):
    block = sources_hbm.shape[0] // blocks
    copies = []
    for number in range(blocks):
        span = pl.ds(number * block, block)
        wanted = sources_hbm.at[span, pl.ds(first, held.shape[1])]
        copies.append(
            (
                pltpu.make_async_copy(encoder_hbm.at[:, span], table.at[:, span], sems.at[0, number]),
                pltpu.make_async_copy(wanted, held.at[span], sems.at[1, number]),
            )
        )
        for copy in copies[-1]:
            copy.start()
    return copies


def add_up(copies, scale_ref, held, table, acc_ref):
    block = held.shape[0] // len(copies)
    for number, pair in enumerate(copies):
        for copy in pair:
            copy.wait()
        span = slice(number * block, (number + 1) * block)
        scaled = (table[:, span].astype(jnp.float32) * scale_ref[:, span]).astype(jnp.bfloat16)
        part = mm(scaled, held[span, :])
        if number == 0:
            acc_ref[...] = part
        else:
            acc_ref[...] += part


def encode_kernel(
    blocks, first, sources_hbm, scale_hbm, encoder_hbm, comp_hbm, exp_hbm, out_ref, held, table, acc_ref, sems, scale_ref, comp_ref, exp_ref, small
):
    pairs = ((scale_hbm, scale_ref), (comp_hbm, comp_ref), (exp_hbm, exp_ref))
    first_copies = [pltpu.make_async_copy(*pair, small.at[number]) for number, pair in enumerate(pairs)]
    for copy in first_copies:
        copy.start()
    copies = start_loads(blocks, first, sources_hbm, encoder_hbm, held, table, sems)
    for copy in first_copies:
        copy.wait()
    parts, rows, _ = out_ref.shape
    own = [comp_ref[number, pl.ds(lax.axis_index("col"), 1), :] for number in range(comp_ref.shape[0])]
    own += [exp_ref[number, pl.ds(lax.axis_index("row"), 1), :] for number in range(exp_ref.shape[0] - 1)]
    gains = [half for gain in own for half in (gain[:, :LANES], gain[:, LANES:])]
    pad = -(-len(gains) // 8) * 8
    gains += [jnp.zeros((1, LANES), jnp.float32)] * (pad - len(gains))
    gains = jnp.concatenate(gains, axis=0).astype(jnp.bfloat16)
    width = (rows - pad) // 2
    add_up(copies, scale_ref, held, table, acc_ref)
    turned = acc_ref[...].T.reshape(parts, width, 2 * LANES)
    out_ref[:, :width, :] = turned[:, :, :LANES].astype(jnp.bfloat16)
    out_ref[:, width : 2 * width, :] = turned[:, :, LANES:].astype(jnp.bfloat16)
    out_ref[:, 2 * width :, :] = jnp.broadcast_to(gains[None], (parts, pad, LANES))


def encode(sources, enc_scale, encoder, comp_gain, exp_gain, parts, first):
    points, width = sources.shape
    width -= first
    skeleton = encoder.shape[0]
    pad = gain_rows(comp_gain, exp_gain)
    blocks = 8
    return pl.pallas_call(
        functools.partial(encode_kernel, blocks, first),
        in_specs=[HBM] * 5,
        compiler_params=pltpu.CompilerParams(vmem_limit_bytes=20 * 2**20),
        out_specs=VMEM,
        out_shape=jax.ShapeDtypeStruct((parts, 2 * (width // parts) + pad, LANES), jnp.bfloat16),
        scratch_shapes=[
            pltpu.VMEM((points, width), jnp.bfloat16),
            pltpu.VMEM((skeleton, points), jnp.bfloat16),
            pltpu.VMEM((skeleton, width), jnp.float32),
            pltpu.SemaphoreType.DMA((2, blocks)),
            pltpu.VMEM((1, points), jnp.float32),
            pltpu.VMEM(comp_gain.shape, jnp.float32),
            pltpu.VMEM(exp_gain.shape, jnp.float32),
            pltpu.SemaphoreType.DMA((3,)),
        ],
    )(sources, in_hbm(enc_scale.reshape(1, points)), encoder, in_hbm(comp_gain), in_hbm(exp_gain))


def side_encode_kernel(blocks, sources_hbm, scale_ref, encoder_hbm, out_ref, held, table, acc_ref, sems):
    copies = start_loads(blocks, 0, sources_hbm, encoder_hbm, held, table, sems)
    add_up(copies, scale_ref, held, table, acc_ref)
    out_ref[...] = acc_ref[...].astype(jnp.bfloat16)


def side_encode(sources, enc_scale, encoder, width):
    points = sources.shape[0]
    skeleton = encoder.shape[0]
    blocks = 8
    return pl.pallas_call(
        functools.partial(side_encode_kernel, blocks),
        in_specs=[HBM, VMEM, HBM],
        compiler_params=pltpu.CompilerParams(vmem_limit_bytes=12 * 2**20),
        out_specs=VMEM,
        out_shape=jax.ShapeDtypeStruct((skeleton, width), jnp.bfloat16),
        scratch_shapes=[
            pltpu.VMEM((points, width), jnp.bfloat16),
            pltpu.VMEM((skeleton, points), jnp.bfloat16),
            pltpu.VMEM((skeleton, width), jnp.float32),
            pltpu.SemaphoreType.DMA((2, blocks)),
        ],
    )(sources, enc_scale.reshape(1, points), encoder)


def side_level_kernel(axis, bit, number, scaled, own_ref, partner_ref, transfer_ref, gain_ref, out_ref):
    skeleton = own_ref.shape[0]
    position = lax.axis_index(axis)
    upper = position // 2**bit % 2
    here = pl.multiple_of(upper * skeleton, skeleton)
    there = pl.multiple_of((1 - upper) * skeleton, skeleton)
    rows = pl.ds(here, skeleton)
    mixed = mm(transfer_ref[number, rows, pl.ds(here, skeleton)], own_ref[...])
    mixed += mm(transfer_ref[number, rows, pl.ds(there, skeleton)], partner_ref[...])
    if scaled:
        gain = jnp.broadcast_to(gain_ref[number, pl.ds(position, 1), :], (8, skeleton)).T
        mixed *= gain[:, :1]
    out_ref[...] = mixed.astype(jnp.bfloat16)


def side_level(own, axis, bit, number, scaled, transfer, gain):
    pairs = [(source, source ^ 2**bit) for source in range(lax.axis_size(axis))]
    partner = lax.ppermute(own, axis, pairs)
    return pl.pallas_call(
        functools.partial(side_level_kernel, axis, bit, number, scaled),
        in_specs=[VMEM] * 4,
        compiler_params=pltpu.CompilerParams(vmem_limit_bytes=8 * 2**20),
        out_specs=VMEM,
        out_shape=jax.ShapeDtypeStruct(own.shape, jnp.bfloat16),
    )(on_chip(own), on_chip(partner), transfer, gain)


def gain_rows(comp_gain, exp_gain):
    sent = 2 * (comp_gain.shape[0] + exp_gain.shape[0] - 1)
    return -(-sent // 8) * 8


def levels_kernel(strides, pad, packed_ref, comp_ref, exp_ref, out_ref):
    boxes, rows, _ = packed_ref.shape
    width = (rows - pad) // 2
    skeleton = 2 * LANES
    state = jnp.concatenate([packed_ref[:, :width, :], packed_ref[:, width : 2 * width, :]], axis=-1)
    state = state.astype(jnp.float32)
    gains = packed_ref[:, 2 * width :, :].astype(jnp.float32)
    for number, stride in enumerate(strides):
        turned = number >= comp_ref.shape[0]
        transfer = exp_ref[number - comp_ref.shape[0]] if turned else comp_ref[number]
        halves = state.reshape(boxes // (2 * stride), 2, stride * width, skeleton)
        low = halves[:, 0].reshape(boxes // 2 * width, skeleton).astype(jnp.bfloat16)
        high = halves[:, 1].reshape(boxes // 2 * width, skeleton).astype(jnp.bfloat16)
        mixed = mm(low, transfer[:, :skeleton], NT) + mm(high, transfer[:, skeleton:], NT)
        shape = (boxes // (2 * stride), 1, stride, width, skeleton)
        state = jnp.concatenate(
            [mixed[:, :skeleton].reshape(shape), mixed[:, skeleton:].reshape(shape)], axis=1
        ).reshape(boxes, width, skeleton)
        if number + 1 < len(strides):
            gain = jnp.concatenate(
                [gains[:, 2 * number : 2 * number + 1, :], gains[:, 2 * number + 1 : 2 * number + 2, :]],
                axis=-1,
            )
            state = state * gain
    out_ref[:, :width, :] = state[:, :, :LANES].astype(jnp.bfloat16)
    out_ref[:, width:, :] = state[:, :, LANES:].astype(jnp.bfloat16)


def levels(packed, comp_transfer, exp_transfer, strides, pad):
    boxes, rows, _ = packed.shape
    return pl.pallas_call(
        functools.partial(levels_kernel, strides, pad),
        in_specs=[VMEM] * 3,
        compiler_params=pltpu.CompilerParams(vmem_limit_bytes=20 * 2**20),
        out_specs=VMEM,
        out_shape=jax.ShapeDtypeStruct((boxes, rows - pad, LANES), jnp.bfloat16),
    )(on_chip(packed), comp_transfer, exp_transfer)


def decode_kernel(blocks, side_ref, packed_ref, decoder_ref, out_hbm, turned_ref, held, sems):
    boxes, rows, _ = packed_ref.shape
    width, side = rows // 2, side_ref.shape[1]
    coeffs = jnp.concatenate([packed_ref[:, :width, :], packed_ref[:, width:, :]], axis=-1)
    coeffs = coeffs.astype(jnp.float32).reshape(boxes * width, 2 * LANES)
    turned_ref[:, :side] = side_ref[...]
    turned_ref[:, side:] = coeffs.T.astype(jnp.bfloat16)
    block = decoder_ref.shape[0] // blocks
    copies = []
    for number in range(blocks):
        span = pl.ds(number * block, block)
        rows_of = slice(number * block, (number + 1) * block)
        held[rows_of, :] = mm(decoder_ref[rows_of, :], turned_ref[...]).astype(jnp.bfloat16)
        copies.append(pltpu.make_async_copy(held.at[span], out_hbm.at[span], sems.at[number]))
        copies[-1].start()
    for copy in copies:
        copy.wait()


def decode(side, packed, decoder):
    boxes, rows, _ = packed.shape
    points, skeleton = decoder.shape
    width = side.shape[1] + boxes * rows // 2
    blocks = 8
    return pl.pallas_call(
        functools.partial(decode_kernel, blocks),
        in_specs=[VMEM, VMEM, VMEM],
        compiler_params=pltpu.CompilerParams(vmem_limit_bytes=20 * 2**20),
        out_specs=HBM,
        out_shape=jax.ShapeDtypeStruct((points, width), jnp.bfloat16),
        scratch_shapes=[
            pltpu.VMEM((skeleton, width), jnp.bfloat16),
            pltpu.VMEM((points, width), jnp.bfloat16),
            pltpu.SemaphoreType.DMA((blocks,)),
        ],
    )(on_chip(side), on_chip(packed), decoder)


def plain_encode(sources, enc_scale, encoder, comp_gain, exp_gain, parts):
    own_comp = lax.dynamic_index_in_dim(comp_gain, lax.axis_index("col"), 1, keepdims=False)
    own_exp = lax.dynamic_index_in_dim(exp_gain, lax.axis_index("row"), 1, keepdims=False)
    gains = jnp.concatenate([own_comp, own_exp[:-1]], axis=0).astype(jnp.bfloat16).reshape(-1, LANES)
    gains = jnp.pad(gains, ((0, gain_rows(comp_gain, exp_gain) - gains.shape[0]), (0, 0)))
    scaled = (encoder.astype(jnp.float32) * enc_scale[None, :]).astype(jnp.bfloat16)
    coeffs = mm(sources, scaled, (((0,), (1,)), ((), ()))).astype(jnp.bfloat16)
    coeffs = coeffs.reshape(parts, -1, 2, LANES).swapaxes(1, 2).reshape(parts, -1, LANES)
    gains = jnp.broadcast_to(gains[None], (parts, *gains.shape))
    return jnp.concatenate([coeffs, gains], axis=1)


def plain_levels(packed, comp_transfer, exp_transfer, strides, pad):
    boxes, rows, _ = packed.shape
    width = (rows - pad) // 2
    skeleton = 2 * LANES
    state = packed[:, : 2 * width].reshape(boxes, 2, width, LANES).swapaxes(1, 2).reshape(boxes, width, skeleton)
    gains = packed[:, 2 * width :].astype(jnp.float32).reshape(boxes, pad // 2, 1, skeleton)
    transfers = jnp.concatenate([comp_transfer, exp_transfer], axis=0)
    for number, stride in enumerate(strides):
        halves = state.reshape(boxes // (2 * stride), 2, stride, width, skeleton)
        stacked = jnp.concatenate([halves[:, 0], halves[:, 1]], axis=-1)
        paired = transfers[number].reshape(2, skeleton, 2 * skeleton)
        both = jnp.einsum("hlsk,tjk->htlsj", stacked, paired, preferred_element_type=jnp.float32)
        both = both.reshape(boxes, width, skeleton)
        if number + 1 < len(strides):
            both = both * gains[:, number]
        state = both.astype(jnp.bfloat16)
    return state.reshape(boxes, width, 2, LANES).swapaxes(1, 2).reshape(boxes, 2 * width, LANES)


def plain_decode(packed, decoder):
    boxes, rows, _ = packed.shape
    width = rows // 2
    coeffs = packed.reshape(boxes, 2, width, LANES).swapaxes(1, 2).reshape(boxes * width, 2 * LANES)
    return mm(decoder, coeffs, NT).astype(jnp.bfloat16)


def body(
    sources,
    enc_scale,
    encoder,
    comp_transfer,
    comp_gain,
    exp_transfer,
    exp_gain,
    decoder,
    dec_scale,
):
    col_count, row_count = lax.axis_size("col"), lax.axis_size("row")
    parts = col_count * row_count
    skeleton = encoder.shape[0]
    comp_levels, exp_levels = comp_transfer.shape[0], exp_transfer.shape[0]
    strides = tuple(row_count * 2**number for number in range(comp_levels)) + tuple(
        2**number for number in range(exp_levels)
    )
    comp_gain, exp_gain = comp_gain[:, 0], exp_gain[:, 0]
    pad = gain_rows(comp_gain, exp_gain)
    last_gain = lax.dynamic_index_in_dim(exp_gain[-1], lax.axis_index("row"), 0, keepdims=False)
    factors = dec_scale[:, None] * last_gain[None, :]
    width = sources.shape[1]
    side = width // 4

    if side % LANES or (width - side) % (8 * parts) or skeleton != 2 * LANES:
        packed = plain_encode(sources, enc_scale, encoder, comp_gain, exp_gain, parts)
        packed = lax.all_to_all(packed, AXES, 0, 0, tiled=True)
        packed = plain_levels(packed, comp_transfer, exp_transfer, strides, pad)
        packed = lax.all_to_all(packed, AXES, 0, 0, tiled=True)
        return plain_decode(packed, (decoder.astype(jnp.float32) * factors).astype(jnp.bfloat16))

    comp_transfer, exp_transfer = on_chip(comp_transfer), on_chip(exp_transfer)
    sources, encoder = in_hbm(sources), in_hbm(encoder)
    packed = encode(sources, enc_scale, encoder, comp_gain, exp_gain, parts, side)
    packed = lax.all_to_all(packed, AXES, 0, 0, tiled=True)
    coeffs = side_encode(sources, enc_scale, encoder, side)
    for number in range(comp_levels):
        coeffs = side_level(coeffs, "col", number, number, True, comp_transfer, comp_gain)
    packed = levels(packed, comp_transfer, exp_transfer, strides, pad)
    packed = lax.all_to_all(packed, AXES, 0, 0, tiled=True)
    for number in range(exp_levels):
        scaled = number + 1 < exp_levels
        coeffs = side_level(coeffs, "row", number, number, scaled, exp_transfer, exp_gain)
    scaled = on_chip((decoder.astype(jnp.float32) * factors).astype(jnp.bfloat16))
    return decode(coeffs, packed, scaled)


def solution(mesh):
    in_specs = (
        P(AXES, None),
        P(AXES),
        P(),
        P(),
        P(None, "row", None, None),
        P(),
        P(None, "col", None, None),
        P(),
        P(AXES),
    )

    def step(*args):
        return jax.shard_map(body, mesh=mesh, in_specs=in_specs, out_specs=P(AXES, None), check_vma=False)(*args)

    return step
```

```python
import functools

import jax
import jax.numpy as jnp
from jax import lax
from jax.experimental import pallas as pl
from jax.experimental.pallas import tpu as pltpu
from jax.sharding import PartitionSpec as P


AXES = ("col", "row")
LANES = 128
NT = (((1,), (1,)), ((), ()))
HBM = pl.BlockSpec(memory_space=pltpu.HBM)
VMEM = pl.BlockSpec(memory_space=pltpu.VMEM)


def on_chip(value):
    return pltpu.with_memory_space_constraint(value, pltpu.VMEM)


def in_hbm(value):
    return pltpu.with_memory_space_constraint(value, pltpu.HBM)


def mm(a, b, dims=(((1,), (0,)), ((), ()))):
    return lax.dot_general(a, b, dims, preferred_element_type=jnp.float32)


def encode_kernel(
    blocks,
    sources_hbm,
    scale_hbm,
    encoder_hbm,
    comp_hbm,
    exp_hbm,
    side_ref,
    out_hbm,
    held,
    table,
    acc_ref,
    sems,
    scale_ref,
    comp_ref,
    exp_ref,
    out_ref,
    small,
):
    pairs = ((scale_hbm, scale_ref), (comp_hbm, comp_ref), (exp_hbm, exp_ref))
    first_copies = [pltpu.make_async_copy(*pair, small.at[number]) for number, pair in enumerate(pairs)]
    for copy in first_copies:
        copy.start()
    block = sources_hbm.shape[0] // blocks
    copies = []
    for number in range(blocks):
        span = pl.ds(number * block, block)
        copies.append(
            (
                pltpu.make_async_copy(encoder_hbm.at[:, span], table.at[:, span], sems.at[0, number]),
                pltpu.make_async_copy(sources_hbm.at[span], held.at[span], sems.at[1, number]),
            )
        )
        for copy in copies[-1]:
            copy.start()
    for copy in first_copies:
        copy.wait()
    for number, pair in enumerate(copies):
        for copy in pair:
            copy.wait()
        span = slice(number * block, (number + 1) * block)
        scaled = (table[:, span].astype(jnp.float32) * scale_ref[:, span]).astype(jnp.bfloat16)
        part = mm(scaled, held[span, :])
        if number == 0:
            acc_ref[...] = part
        else:
            acc_ref[...] += part

    own = [comp_ref[number, pl.ds(lax.axis_index("col"), 1), :] for number in range(comp_ref.shape[0])]
    own += [exp_ref[number, pl.ds(lax.axis_index("row"), 1), :] for number in range(exp_ref.shape[0] - 1)]
    gains = [half for gain in own for half in (gain[:, :LANES], gain[:, LANES:])]
    pad = -(-len(gains) // 8) * 8
    gains += [jnp.zeros((1, LANES), jnp.float32)] * (pad - len(gains))
    gains = jnp.concatenate(gains, axis=0)
    parts, rows, _ = out_ref.shape
    width, side = (rows - pad) // 2, side_ref.shape[1]
    side_ref[...] = acc_ref[:, :side].astype(jnp.bfloat16)
    turned = acc_ref[:, side:].T.reshape(parts, width, 2 * LANES)
    gains = jnp.broadcast_to(gains[None], (parts, pad, LANES))
    joined = jnp.concatenate([turned[:, :, :LANES], turned[:, :, LANES:], gains], axis=1)
    out_ref[...] = joined.astype(jnp.bfloat16)
    copy = pltpu.make_async_copy(out_ref, out_hbm, small.at[len(pairs)])
    copy.start()
    copy.wait()


def encode(sources, enc_scale, encoder, comp_gain, exp_gain, parts, side):
    points, width = sources.shape
    skeleton = encoder.shape[0]
    pad = gain_rows(comp_gain, exp_gain)
    packed = (parts, 2 * ((width - side) // parts) + pad, LANES)
    blocks = 8
    return pl.pallas_call(
        functools.partial(encode_kernel, blocks),
        in_specs=[HBM] * 5,
        out_specs=[VMEM, HBM],
        compiler_params=pltpu.CompilerParams(vmem_limit_bytes=24 * 2**20),
        out_shape=[jax.ShapeDtypeStruct((skeleton, side), jnp.bfloat16), pltpu.HBM(packed, jnp.bfloat16)],
        scratch_shapes=[
            pltpu.VMEM((points, width), jnp.bfloat16),
            pltpu.VMEM((skeleton, points), jnp.bfloat16),
            pltpu.VMEM((skeleton, width), jnp.float32),
            pltpu.SemaphoreType.DMA((2, blocks)),
            pltpu.VMEM((1, points), jnp.float32),
            pltpu.VMEM(comp_gain.shape, jnp.float32),
            pltpu.VMEM(exp_gain.shape, jnp.float32),
            pltpu.VMEM(packed, jnp.bfloat16),
            pltpu.SemaphoreType.DMA((4,)),
        ],
    )(sources, in_hbm(enc_scale.reshape(1, points)), encoder, in_hbm(comp_gain), in_hbm(exp_gain))


def side_level_kernel(axis, bit, number, scaled, own_ref, partner_ref, transfer_ref, gain_ref, out_ref):
    skeleton = own_ref.shape[0]
    position = lax.axis_index(axis)
    upper = position // 2**bit % 2
    here = pl.multiple_of(upper * skeleton, skeleton)
    there = pl.multiple_of((1 - upper) * skeleton, skeleton)
    rows = pl.ds(here, skeleton)
    mixed = mm(transfer_ref[number, rows, pl.ds(here, skeleton)], own_ref[...])
    mixed += mm(transfer_ref[number, rows, pl.ds(there, skeleton)], partner_ref[...])
    if scaled:
        gain = jnp.broadcast_to(gain_ref[number, pl.ds(position, 1), :], (8, skeleton)).T
        mixed *= gain[:, :1]
    out_ref[...] = mixed.astype(jnp.bfloat16)


def side_level(own, axis, bit, number, scaled, transfer, gain):
    pairs = [(source, source ^ 2**bit) for source in range(lax.axis_size(axis))]
    partner = lax.ppermute(own, axis, pairs)
    return pl.pallas_call(
        functools.partial(side_level_kernel, axis, bit, number, scaled),
        in_specs=[VMEM] * 4,
        compiler_params=pltpu.CompilerParams(vmem_limit_bytes=8 * 2**20),
        out_specs=VMEM,
        out_shape=jax.ShapeDtypeStruct(own.shape, jnp.bfloat16),
    )(on_chip(own), on_chip(partner), transfer, gain)


def gain_rows(comp_gain, exp_gain):
    sent = 2 * (comp_gain.shape[0] + exp_gain.shape[0] - 1)
    return -(-sent // 8) * 8


def levels_kernel(strides, pad, packed_ref, comp_ref, exp_ref, out_ref):
    boxes, rows, _ = packed_ref.shape
    width = (rows - pad) // 2
    skeleton = 2 * LANES
    packed = packed_ref[...].astype(jnp.float32)
    state = jnp.concatenate([packed[:, :width, :], packed[:, width : 2 * width, :]], axis=-1)
    gains = packed[:, 2 * width :, :]
    for number, stride in enumerate(strides):
        turned = number >= comp_ref.shape[0]
        transfer = exp_ref[number - comp_ref.shape[0]] if turned else comp_ref[number]
        halves = state.reshape(boxes // (2 * stride), 2, stride * width, skeleton)
        low = halves[:, 0].reshape(boxes // 2 * width, skeleton).astype(jnp.bfloat16)
        high = halves[:, 1].reshape(boxes // 2 * width, skeleton).astype(jnp.bfloat16)
        mixed = mm(low, transfer[:, :skeleton], NT) + mm(high, transfer[:, skeleton:], NT)
        shape = (boxes // (2 * stride), 1, stride, width, skeleton)
        state = jnp.concatenate(
            [mixed[:, :skeleton].reshape(shape), mixed[:, skeleton:].reshape(shape)], axis=1
        ).reshape(boxes, width, skeleton)
        if number + 1 < len(strides):
            gain = jnp.concatenate(
                [gains[:, 2 * number : 2 * number + 1, :], gains[:, 2 * number + 1 : 2 * number + 2, :]],
                axis=-1,
            )
            state = state * gain
    out_ref[...] = jnp.concatenate([state[:, :, :LANES], state[:, :, LANES:]], axis=1).astype(jnp.bfloat16)


def levels(packed, comp_transfer, exp_transfer, strides, pad):
    boxes, rows, _ = packed.shape
    return pl.pallas_call(
        functools.partial(levels_kernel, strides, pad),
        in_specs=[VMEM] * 3,
        compiler_params=pltpu.CompilerParams(vmem_limit_bytes=20 * 2**20),
        out_specs=VMEM,
        out_shape=jax.ShapeDtypeStruct((boxes, rows - pad, LANES), jnp.bfloat16),
    )(on_chip(packed), comp_transfer, exp_transfer)


def table_kernel(decoder_ref, scale_ref, gain_ref, out_ref):
    gain = gain_ref[gain_ref.shape[0] - 1, pl.ds(lax.axis_index("row"), 1), :]
    count = scale_ref.shape[0]
    scales = scale_ref[...].T
    for number in range(count):
        rows = slice(number * LANES, (number + 1) * LANES)
        factors = scales[:, number : number + 1] * gain
        out_ref[rows, :] = (decoder_ref[rows, :].astype(jnp.float32) * factors).astype(jnp.bfloat16)


def scaled_table(decoder, dec_scale, exp_gain):
    return pl.pallas_call(
        table_kernel,
        in_specs=[VMEM] * 3,
        out_specs=VMEM,
        compiler_params=pltpu.CompilerParams(vmem_limit_bytes=8 * 2**20),
        out_shape=jax.ShapeDtypeStruct(decoder.shape, jnp.bfloat16),
    )(decoder, dec_scale.reshape(-1, LANES), exp_gain)


def decode_kernel(blocks, side_ref, packed_ref, decoder_hbm, out_hbm, turned_ref, held, decoder_ref, sems):
    block = decoder_ref.shape[0] // blocks
    loads = []
    for number in range(blocks):
        span = pl.ds(number * block, block)
        loads.append(pltpu.make_async_copy(decoder_hbm.at[span], decoder_ref.at[span], sems.at[0, number]))
        loads[-1].start()
    boxes, rows, _ = packed_ref.shape
    width, side = rows // 2, side_ref.shape[1]
    packed = packed_ref[...].astype(jnp.float32)
    coeffs = jnp.concatenate([packed[:, :width, :], packed[:, width:, :]], axis=-1)
    coeffs = coeffs.reshape(boxes * width, 2 * LANES)
    turned_ref[:, :side] = side_ref[...]
    turned_ref[:, side:] = coeffs.T.astype(jnp.bfloat16)
    copies = []
    for number in range(blocks):
        loads[number].wait()
        span = pl.ds(number * block, block)
        rows_of = slice(number * block, (number + 1) * block)
        held[rows_of, :] = mm(decoder_ref[rows_of, :], turned_ref[...]).astype(jnp.bfloat16)
        copies.append(pltpu.make_async_copy(held.at[span], out_hbm.at[span], sems.at[1, number]))
        copies[-1].start()
    for copy in copies:
        copy.wait()


def decode(side, packed, decoder):
    boxes, rows, _ = packed.shape
    points, skeleton = decoder.shape
    width = side.shape[1] + boxes * rows // 2
    blocks = 8
    return pl.pallas_call(
        functools.partial(decode_kernel, blocks),
        in_specs=[VMEM, VMEM, HBM],
        compiler_params=pltpu.CompilerParams(vmem_limit_bytes=20 * 2**20),
        out_specs=HBM,
        out_shape=jax.ShapeDtypeStruct((points, width), jnp.bfloat16),
        scratch_shapes=[
            pltpu.VMEM((skeleton, width), jnp.bfloat16),
            pltpu.VMEM((points, width), jnp.bfloat16),
            pltpu.VMEM((points, skeleton), jnp.bfloat16),
            pltpu.SemaphoreType.DMA((2, blocks)),
        ],
    )(on_chip(side), on_chip(packed), in_hbm(decoder))


def plain_encode(sources, enc_scale, encoder, comp_gain, exp_gain, parts):
    own_comp = lax.dynamic_index_in_dim(comp_gain, lax.axis_index("col"), 1, keepdims=False)
    own_exp = lax.dynamic_index_in_dim(exp_gain, lax.axis_index("row"), 1, keepdims=False)
    gains = jnp.concatenate([own_comp, own_exp[:-1]], axis=0).astype(jnp.bfloat16).reshape(-1, LANES)
    gains = jnp.pad(gains, ((0, gain_rows(comp_gain, exp_gain) - gains.shape[0]), (0, 0)))
    scaled = (encoder.astype(jnp.float32) * enc_scale[None, :]).astype(jnp.bfloat16)
    coeffs = mm(sources, scaled, (((0,), (1,)), ((), ()))).astype(jnp.bfloat16)
    coeffs = coeffs.reshape(parts, -1, 2, LANES).swapaxes(1, 2).reshape(parts, -1, LANES)
    gains = jnp.broadcast_to(gains[None], (parts, *gains.shape))
    return jnp.concatenate([coeffs, gains], axis=1)


def plain_levels(packed, comp_transfer, exp_transfer, strides, pad):
    boxes, rows, _ = packed.shape
    width = (rows - pad) // 2
    skeleton = 2 * LANES
    state = packed[:, : 2 * width].reshape(boxes, 2, width, LANES).swapaxes(1, 2).reshape(boxes, width, skeleton)
    gains = packed[:, 2 * width :].astype(jnp.float32).reshape(boxes, pad // 2, 1, skeleton)
    transfers = jnp.concatenate([comp_transfer, exp_transfer], axis=0)
    for number, stride in enumerate(strides):
        halves = state.reshape(boxes // (2 * stride), 2, stride, width, skeleton)
        stacked = jnp.concatenate([halves[:, 0], halves[:, 1]], axis=-1)
        paired = transfers[number].reshape(2, skeleton, 2 * skeleton)
        both = jnp.einsum("hlsk,tjk->htlsj", stacked, paired, preferred_element_type=jnp.float32)
        both = both.reshape(boxes, width, skeleton)
        if number + 1 < len(strides):
            both = both * gains[:, number]
        state = both.astype(jnp.bfloat16)
    return state.reshape(boxes, width, 2, LANES).swapaxes(1, 2).reshape(boxes, 2 * width, LANES)


def plain_decode(packed, decoder):
    boxes, rows, _ = packed.shape
    width = rows // 2
    coeffs = packed.reshape(boxes, 2, width, LANES).swapaxes(1, 2).reshape(boxes * width, 2 * LANES)
    return mm(decoder, coeffs, NT).astype(jnp.bfloat16)


def body(
    sources,
    enc_scale,
    encoder,
    comp_transfer,
    comp_gain,
    exp_transfer,
    exp_gain,
    decoder,
    dec_scale,
):
    col_count, row_count = lax.axis_size("col"), lax.axis_size("row")
    parts = col_count * row_count
    skeleton = encoder.shape[0]
    comp_levels, exp_levels = comp_transfer.shape[0], exp_transfer.shape[0]
    strides = tuple(row_count * 2**number for number in range(comp_levels)) + tuple(
        2**number for number in range(exp_levels)
    )
    comp_gain, exp_gain = comp_gain[:, 0], exp_gain[:, 0]
    pad = gain_rows(comp_gain, exp_gain)
    last_gain = lax.dynamic_index_in_dim(exp_gain[-1], lax.axis_index("row"), 0, keepdims=False)
    factors = dec_scale[:, None] * last_gain[None, :]
    width = sources.shape[1]
    side = width // 4

    if side % LANES or (width - side) % (8 * parts) or skeleton != 2 * LANES:
        packed = plain_encode(sources, enc_scale, encoder, comp_gain, exp_gain, parts)
        packed = lax.all_to_all(packed, AXES, 0, 0, tiled=True)
        packed = plain_levels(packed, comp_transfer, exp_transfer, strides, pad)
        packed = lax.all_to_all(packed, AXES, 0, 0, tiled=True)
        return plain_decode(packed, (decoder.astype(jnp.float32) * factors).astype(jnp.bfloat16))

    comp_transfer, exp_transfer = on_chip(comp_transfer), on_chip(exp_transfer)
    sources, encoder = in_hbm(sources), in_hbm(encoder)
    coeffs, packed = encode(sources, enc_scale, encoder, comp_gain, exp_gain, parts, side)
    packed = lax.all_to_all(packed, AXES, 0, 0, tiled=True)
    for number in range(comp_levels):
        coeffs = side_level(coeffs, "col", number, number, True, comp_transfer, comp_gain)
    table = scaled_table(decoder, dec_scale, exp_gain)
    packed = levels(packed, comp_transfer, exp_transfer, strides, pad)
    packed = lax.all_to_all(packed, AXES, 0, 0, tiled=True)
    for number in range(exp_levels):
        scaled = number + 1 < exp_levels
        coeffs = side_level(coeffs, "row", number, number, scaled, exp_transfer, exp_gain)
    return decode(coeffs, packed, table)


def solution(mesh):
    in_specs = (
        P(AXES, None),
        P(AXES),
        P(),
        P(),
        P(None, "row", None, None),
        P(),
        P(None, "col", None, None),
        P(),
        P(AXES),
    )

    def step(*args):
        return jax.shard_map(body, mesh=mesh, in_specs=in_specs, out_specs=P(AXES, None), check_vma=False)(*args)

    return step
```

```python
import functools

import jax
import jax.numpy as jnp
from jax import lax
from jax.experimental import pallas as pl
from jax.experimental.pallas import tpu as pltpu
from jax.sharding import PartitionSpec as P


AXES = ("col", "row")
ORDER = ("row", "col")
LANES = 128
NT = (((1,), (1,)), ((), ()))
HBM = pl.BlockSpec(memory_space=pltpu.HBM)
VMEM = pl.BlockSpec(memory_space=pltpu.VMEM)


def on_chip(value):
    return pltpu.with_memory_space_constraint(value, pltpu.VMEM)


def in_hbm(value):
    return pltpu.with_memory_space_constraint(value, pltpu.HBM)


def mm(a, b, dims=(((1,), (0,)), ((), ()))):
    return lax.dot_general(a, b, dims, preferred_element_type=jnp.float32)


def start_loads(blocks, first, sources_hbm, encoder_hbm, held, table, sems):
    block = sources_hbm.shape[0] // blocks
    copies = []
    for number in range(blocks):
        span = pl.ds(number * block, block)
        wanted = sources_hbm.at[span, pl.ds(first, held.shape[1])]
        copies.append(
            (
                pltpu.make_async_copy(encoder_hbm.at[:, span], table.at[:, span], sems.at[0, number]),
                pltpu.make_async_copy(wanted, held.at[span], sems.at[1, number]),
            )
        )
        for copy in copies[-1]:
            copy.start()
    return copies


def add_up(copies, scale_ref, held, table, acc_ref):
    block = held.shape[0] // len(copies)
    for number, pair in enumerate(copies):
        for copy in pair:
            copy.wait()
        span = slice(number * block, (number + 1) * block)
        scaled = (table[:, span].astype(jnp.float32) * scale_ref[:, span]).astype(jnp.bfloat16)
        part = mm(scaled, held[span, :])
        if number == 0:
            acc_ref[...] = part
        else:
            acc_ref[...] += part


def encode_kernel(
    blocks,
    first,
    sources_hbm,
    scale_hbm,
    encoder_hbm,
    comp_hbm,
    exp_hbm,
    out_hbm,
    held,
    table,
    acc_ref,
    sems,
    scale_ref,
    comp_ref,
    exp_ref,
    out_ref,
    small,
):
    pairs = ((scale_hbm, scale_ref), (comp_hbm, comp_ref), (exp_hbm, exp_ref))
    first_copies = [pltpu.make_async_copy(*pair, small.at[number]) for number, pair in enumerate(pairs)]
    for copy in first_copies:
        copy.start()
    copies = start_loads(blocks, first, sources_hbm, encoder_hbm, held, table, sems)
    for copy in first_copies:
        copy.wait()
    add_up(copies, scale_ref, held, table, acc_ref)
    own = [comp_ref[number, pl.ds(lax.axis_index("col"), 1), :] for number in range(comp_ref.shape[0])]
    own += [exp_ref[number, pl.ds(lax.axis_index("row"), 1), :] for number in range(exp_ref.shape[0] - 1)]
    gains = [half for gain in own for half in (gain[:, :LANES], gain[:, LANES:])]
    pad = -(-len(gains) // 8) * 8
    gains += [jnp.zeros((1, LANES), jnp.float32)] * (pad - len(gains))
    gains = jnp.concatenate(gains, axis=0)
    parts, rows, _ = out_ref.shape
    width = (rows - pad) // 2
    turned = acc_ref[...].T.reshape(parts, width, 2 * LANES)
    gains = jnp.broadcast_to(gains[None], (parts, pad, LANES))
    joined = jnp.concatenate([turned[:, :, :LANES], turned[:, :, LANES:], gains], axis=1)
    out_ref[...] = joined.astype(jnp.bfloat16)
    copy = pltpu.make_async_copy(out_ref, out_hbm, small.at[len(pairs)])
    copy.start()
    copy.wait()


def encode(sources, enc_scale, encoder, comp_gain, exp_gain, parts, first):
    points, width = sources.shape
    width -= first
    skeleton = encoder.shape[0]
    pad = gain_rows(comp_gain, exp_gain)
    packed = (parts, 2 * (width // parts) + pad, LANES)
    blocks = 8
    return pl.pallas_call(
        functools.partial(encode_kernel, blocks, first),
        in_specs=[HBM] * 5,
        out_specs=HBM,
        compiler_params=pltpu.CompilerParams(vmem_limit_bytes=20 * 2**20),
        out_shape=pltpu.HBM(packed, jnp.bfloat16),
        scratch_shapes=[
            pltpu.VMEM((points, width), jnp.bfloat16),
            pltpu.VMEM((skeleton, points), jnp.bfloat16),
            pltpu.VMEM((skeleton, width), jnp.float32),
            pltpu.SemaphoreType.DMA((2, blocks)),
            pltpu.VMEM((1, points), jnp.float32),
            pltpu.VMEM(comp_gain.shape, jnp.float32),
            pltpu.VMEM(exp_gain.shape, jnp.float32),
            pltpu.VMEM(packed, jnp.bfloat16),
            pltpu.SemaphoreType.DMA((4,)),
        ],
    )(sources, in_hbm(enc_scale.reshape(1, points)), encoder, in_hbm(comp_gain), in_hbm(exp_gain))


def side_encode_kernel(blocks, sources_hbm, scale_hbm, encoder_hbm, out_ref, held, table, acc_ref, sems, scale_ref, small):
    first_copy = pltpu.make_async_copy(scale_hbm, scale_ref, small)
    first_copy.start()
    copies = start_loads(blocks, 0, sources_hbm, encoder_hbm, held, table, sems)
    first_copy.wait()
    add_up(copies, scale_ref, held, table, acc_ref)
    out_ref[...] = acc_ref[...].astype(jnp.bfloat16)


def side_encode(sources, enc_scale, encoder, width):
    points = sources.shape[0]
    skeleton = encoder.shape[0]
    blocks = 4
    return pl.pallas_call(
        functools.partial(side_encode_kernel, blocks),
        in_specs=[HBM] * 3,
        out_specs=VMEM,
        compiler_params=pltpu.CompilerParams(vmem_limit_bytes=12 * 2**20),
        out_shape=jax.ShapeDtypeStruct((skeleton, width), jnp.bfloat16),
        scratch_shapes=[
            pltpu.VMEM((points, width), jnp.bfloat16),
            pltpu.VMEM((skeleton, points), jnp.bfloat16),
            pltpu.VMEM((skeleton, width), jnp.float32),
            pltpu.SemaphoreType.DMA((2, blocks)),
            pltpu.VMEM((1, points), jnp.float32),
            pltpu.SemaphoreType.DMA,
        ],
    )(sources, in_hbm(enc_scale.reshape(1, points)), encoder)


def pick_kernel(comp_hbm, exp_hbm, *refs):
    *outs, sems = refs
    copies = []
    for number, out_ref in enumerate(outs):
        level = number - comp_hbm.shape[0]
        source, axis = (comp_hbm.at[number], "col") if level < 0 else (exp_hbm.at[level], "row")
        bit = number if level < 0 else level
        skeleton = out_ref.shape[0]
        here = pl.multiple_of(lax.axis_index(axis) // 2**bit % 2 * skeleton, skeleton)
        copies.append(pltpu.make_async_copy(source.at[pl.ds(here, skeleton)], out_ref, sems.at[number]))
        copies[-1].start()
    for copy in copies:
        copy.wait()


def pick(comp_transfer, exp_transfer):
    count = comp_transfer.shape[0] + exp_transfer.shape[0]
    skeleton = comp_transfer.shape[1] // 2
    return pl.pallas_call(
        pick_kernel,
        in_specs=[HBM] * 2,
        out_specs=[VMEM] * count,
        compiler_params=pltpu.CompilerParams(vmem_limit_bytes=4 * 2**20),
        out_shape=[jax.ShapeDtypeStruct((skeleton, 2 * skeleton), jnp.bfloat16)] * count,
        scratch_shapes=[pltpu.SemaphoreType.DMA((count,))],
    )(in_hbm(comp_transfer), in_hbm(exp_transfer))


def side_level_kernel(axis, bit, scaled, own_ref, partner_ref, rows_ref, gain_ref, out_ref):
    skeleton = own_ref.shape[0]
    position = lax.axis_index(axis)
    upper = position // 2**bit % 2
    here = pl.multiple_of(upper * skeleton, skeleton)
    there = pl.multiple_of((1 - upper) * skeleton, skeleton)
    mixed = mm(rows_ref[:, pl.ds(here, skeleton)], own_ref[...])
    mixed += mm(rows_ref[:, pl.ds(there, skeleton)], partner_ref[...])
    if scaled:
        gain = jnp.broadcast_to(gain_ref[bit, pl.ds(position, 1), :], (8, skeleton)).T
        mixed *= gain[:, :1]
    out_ref[...] = mixed.astype(jnp.bfloat16)


def side_level(own, axis, bit, scaled, rows, gain):
    pairs = [(source, source ^ 2**bit) for source in range(lax.axis_size(axis))]
    partner = lax.ppermute(own, axis, pairs)
    return pl.pallas_call(
        functools.partial(side_level_kernel, axis, bit, scaled),
        in_specs=[VMEM] * 4,
        compiler_params=pltpu.CompilerParams(vmem_limit_bytes=4 * 2**20),
        out_specs=VMEM,
        out_shape=jax.ShapeDtypeStruct(own.shape, jnp.bfloat16),
    )(on_chip(own), on_chip(partner), on_chip(rows), gain)


def gain_rows(comp_gain, exp_gain):
    sent = 2 * (comp_gain.shape[0] + exp_gain.shape[0] - 1)
    return -(-sent // 8) * 8


def levels_kernel(strides, pad, packed_ref, comp_ref, exp_hbm, out_ref, exp_ref, sems):
    copies = []
    for number in range(exp_hbm.shape[0]):
        copies.append(pltpu.make_async_copy(exp_hbm.at[number], exp_ref.at[number], sems.at[number]))
        copies[-1].start()
    boxes, rows, _ = packed_ref.shape
    width = (rows - pad) // 2
    skeleton = 2 * LANES
    packed = packed_ref[...].astype(jnp.float32)
    state = jnp.concatenate([packed[:, :width, :], packed[:, width : 2 * width, :]], axis=-1)
    gains = packed[:, 2 * width :, :]
    for number, stride in enumerate(strides):
        turned = number >= comp_ref.shape[0]
        if turned:
            copies[number - comp_ref.shape[0]].wait()
        transfer = exp_ref[number - comp_ref.shape[0]] if turned else comp_ref[number]
        halves = state.reshape(boxes // (2 * stride), 2, stride * width, skeleton)
        low = halves[:, 0].reshape(boxes // 2 * width, skeleton).astype(jnp.bfloat16)
        high = halves[:, 1].reshape(boxes // 2 * width, skeleton).astype(jnp.bfloat16)
        mixed = mm(low, transfer[:, :skeleton], NT) + mm(high, transfer[:, skeleton:], NT)
        shape = (boxes // (2 * stride), 1, stride, width, skeleton)
        state = jnp.concatenate(
            [mixed[:, :skeleton].reshape(shape), mixed[:, skeleton:].reshape(shape)], axis=1
        ).reshape(boxes, width, skeleton)
        if number + 1 < len(strides):
            gain = jnp.concatenate(
                [gains[:, 2 * number : 2 * number + 1, :], gains[:, 2 * number + 1 : 2 * number + 2, :]],
                axis=-1,
            )
            state = state * gain
    out_ref[...] = jnp.concatenate([state[:, :, :LANES], state[:, :, LANES:]], axis=1).astype(jnp.bfloat16)


def levels(packed, comp_transfer, exp_transfer, strides, pad):
    boxes, rows, _ = packed.shape
    return pl.pallas_call(
        functools.partial(levels_kernel, strides, pad),
        in_specs=[VMEM, VMEM, HBM],
        compiler_params=pltpu.CompilerParams(vmem_limit_bytes=20 * 2**20),
        out_specs=VMEM,
        out_shape=jax.ShapeDtypeStruct((boxes, rows - pad, LANES), jnp.bfloat16),
        scratch_shapes=[
            pltpu.VMEM(exp_transfer.shape, jnp.bfloat16),
            pltpu.SemaphoreType.DMA((exp_transfer.shape[0],)),
        ],
    )(on_chip(packed), on_chip(comp_transfer), in_hbm(exp_transfer))


def decode_kernel(blocks, side_ref, packed_ref, decoder_ref, out_hbm, turned_ref, held, sems):
    boxes, rows, _ = packed_ref.shape
    width, side = rows // 2, side_ref.shape[1]
    packed = packed_ref[...].astype(jnp.float32)
    coeffs = jnp.concatenate([packed[:, :width, :], packed[:, width:, :]], axis=-1)
    coeffs = coeffs.reshape(boxes * width, 2 * LANES)
    turned_ref[:, :side] = side_ref[...]
    turned_ref[:, side:] = coeffs.T.astype(jnp.bfloat16)
    block = decoder_ref.shape[0] // blocks
    copies = []
    for number in range(blocks):
        span = pl.ds(number * block, block)
        rows_of = slice(number * block, (number + 1) * block)
        held[rows_of, :] = mm(decoder_ref[rows_of, :], turned_ref[...]).astype(jnp.bfloat16)
        copies.append(pltpu.make_async_copy(held.at[span], out_hbm.at[span], sems.at[number]))
        copies[-1].start()
    for copy in copies:
        copy.wait()


def decode(side, packed, decoder):
    boxes, rows, _ = packed.shape
    points, skeleton = decoder.shape
    width = side.shape[1] + boxes * rows // 2
    blocks = 8
    return pl.pallas_call(
        functools.partial(decode_kernel, blocks),
        in_specs=[VMEM, VMEM, VMEM],
        compiler_params=pltpu.CompilerParams(vmem_limit_bytes=20 * 2**20),
        out_specs=HBM,
        out_shape=jax.ShapeDtypeStruct((points, width), jnp.bfloat16),
        scratch_shapes=[
            pltpu.VMEM((skeleton, width), jnp.bfloat16),
            pltpu.VMEM((points, width), jnp.bfloat16),
            pltpu.SemaphoreType.DMA((blocks,)),
        ],
    )(on_chip(side), on_chip(packed), decoder)


def plain_encode(sources, enc_scale, encoder, comp_gain, exp_gain, parts):
    own_comp = lax.dynamic_index_in_dim(comp_gain, lax.axis_index("col"), 1, keepdims=False)
    own_exp = lax.dynamic_index_in_dim(exp_gain, lax.axis_index("row"), 1, keepdims=False)
    gains = jnp.concatenate([own_comp, own_exp[:-1]], axis=0).astype(jnp.bfloat16).reshape(-1, LANES)
    gains = jnp.pad(gains, ((0, gain_rows(comp_gain, exp_gain) - gains.shape[0]), (0, 0)))
    scaled = (encoder.astype(jnp.float32) * enc_scale[None, :]).astype(jnp.bfloat16)
    coeffs = mm(sources, scaled, (((0,), (1,)), ((), ()))).astype(jnp.bfloat16)
    coeffs = coeffs.reshape(parts, -1, 2, LANES).swapaxes(1, 2).reshape(parts, -1, LANES)
    gains = jnp.broadcast_to(gains[None], (parts, *gains.shape))
    return jnp.concatenate([coeffs, gains], axis=1)


def plain_levels(packed, comp_transfer, exp_transfer, strides, pad):
    boxes, rows, _ = packed.shape
    width = (rows - pad) // 2
    skeleton = 2 * LANES
    state = packed[:, : 2 * width].reshape(boxes, 2, width, LANES).swapaxes(1, 2).reshape(boxes, width, skeleton)
    gains = packed[:, 2 * width :].astype(jnp.float32).reshape(boxes, pad // 2, 1, skeleton)
    transfers = jnp.concatenate([comp_transfer, exp_transfer], axis=0)
    for number, stride in enumerate(strides):
        halves = state.reshape(boxes // (2 * stride), 2, stride, width, skeleton)
        stacked = jnp.concatenate([halves[:, 0], halves[:, 1]], axis=-1)
        paired = transfers[number].reshape(2, skeleton, 2 * skeleton)
        both = jnp.einsum("hlsk,tjk->htlsj", stacked, paired, preferred_element_type=jnp.float32)
        both = both.reshape(boxes, width, skeleton)
        if number + 1 < len(strides):
            both = both * gains[:, number]
        state = both.astype(jnp.bfloat16)
    return state.reshape(boxes, width, 2, LANES).swapaxes(1, 2).reshape(boxes, 2 * width, LANES)


def plain_decode(packed, decoder):
    boxes, rows, _ = packed.shape
    width = rows // 2
    coeffs = packed.reshape(boxes, 2, width, LANES).swapaxes(1, 2).reshape(boxes * width, 2 * LANES)
    return mm(decoder, coeffs, NT).astype(jnp.bfloat16)


def body(
    sources,
    enc_scale,
    encoder,
    comp_transfer,
    comp_gain,
    exp_transfer,
    exp_gain,
    decoder,
    dec_scale,
):
    col_count, row_count = lax.axis_size("col"), lax.axis_size("row")
    parts = col_count * row_count
    skeleton = encoder.shape[0]
    comp_levels, exp_levels = comp_transfer.shape[0], exp_transfer.shape[0]
    strides = tuple(2**number for number in range(comp_levels))
    strides += tuple(col_count * 2**number for number in range(exp_levels))
    comp_gain, exp_gain = comp_gain[:, 0], exp_gain[:, 0]
    pad = gain_rows(comp_gain, exp_gain)
    last_gain = lax.dynamic_index_in_dim(exp_gain[-1], lax.axis_index("row"), 0, keepdims=False)
    factors = dec_scale[:, None] * last_gain[None, :]
    width = sources.shape[1]
    side = width // 4

    if side % LANES or (width - side) % (8 * parts) or skeleton != 2 * LANES:
        packed = plain_encode(sources, enc_scale, encoder, comp_gain, exp_gain, parts)
        packed = lax.all_to_all(packed, ORDER, 0, 0, tiled=True)
        packed = plain_levels(packed, comp_transfer, exp_transfer, strides, pad)
        packed = lax.all_to_all(packed, ORDER, 0, 0, tiled=True)
        return plain_decode(packed, (decoder.astype(jnp.float32) * factors).astype(jnp.bfloat16))

    sources, encoder = in_hbm(sources), in_hbm(encoder)
    packed = encode(sources, enc_scale, encoder, comp_gain, exp_gain, parts, side)
    packed = lax.all_to_all(packed, ORDER, 0, 0, tiled=True)
    coeffs = side_encode(sources, enc_scale, encoder, side)
    rows = pick(comp_transfer, exp_transfer)
    for number in range(comp_levels):
        coeffs = side_level(coeffs, "col", number, True, rows[number], comp_gain)
    packed = levels(packed, comp_transfer, exp_transfer, strides, pad)
    packed = lax.all_to_all(packed, ORDER, 0, 0, tiled=True)
    for number in range(exp_levels):
        scaled = number + 1 < exp_levels
        coeffs = side_level(coeffs, "row", number, scaled, rows[comp_levels + number], exp_gain)
    table = on_chip((decoder.astype(jnp.float32) * factors).astype(jnp.bfloat16))
    return decode(coeffs, packed, table)


def solution(mesh):
    in_specs = (
        P(AXES, None),
        P(AXES),
        P(),
        P(),
        P(None, "row", None, None),
        P(),
        P(None, "col", None, None),
        P(),
        P(AXES),
    )

    def step(*args):
        return jax.shard_map(body, mesh=mesh, in_specs=in_specs, out_specs=P(AXES, None), check_vma=False)(*args)

    return step
```

```python
import functools

import jax
import jax.numpy as jnp
from jax import lax
from jax.experimental import pallas as pl
from jax.experimental.pallas import tpu as pltpu
from jax.sharding import PartitionSpec as P


AXES = ("col", "row")
ORDER = ("row", "col")
LANES = 128
NT = (((1,), (1,)), ((), ()))
HBM = pl.BlockSpec(memory_space=pltpu.HBM)
VMEM = pl.BlockSpec(memory_space=pltpu.VMEM)


def on_chip(value):
    return pltpu.with_memory_space_constraint(value, pltpu.VMEM)


def in_hbm(value):
    return pltpu.with_memory_space_constraint(value, pltpu.HBM)


def mm(a, b, dims=(((1,), (0,)), ((), ()))):
    return lax.dot_general(a, b, dims, preferred_element_type=jnp.float32)


def add_up(window, loads, multiply, acc_ref):
    for copies in loads[:window]:
        for copy in copies:
            copy.start()
    for number, copies in enumerate(loads):
        for copy in copies:
            copy.wait()
        for copy in loads[number + window] if number + window < len(loads) else ():
            copy.start()
        if number == 0:
            acc_ref[...] = multiply(number)
        else:
            acc_ref[...] += multiply(number)


def encode_kernel(
    blocks,
    first,
    sources_hbm,
    scale_hbm,
    encoder_hbm,
    comp_hbm,
    exp_hbm,
    out_hbm,
    held,
    table,
    acc_ref,
    sems,
    scale_ref,
    comp_ref,
    exp_ref,
    out_ref,
    small,
):
    pairs = ((scale_hbm, scale_ref), (comp_hbm, comp_ref), (exp_hbm, exp_ref))
    first_copies = [pltpu.make_async_copy(*pair, small.at[number]) for number, pair in enumerate(pairs)]
    for copy in first_copies:
        copy.start()
    block = held.shape[0] // blocks
    loads = []
    for number in range(blocks):
        span = pl.ds(number * block, block)
        wanted = sources_hbm.at[span, pl.ds(first, held.shape[1])]
        loads.append(
            (
                pltpu.make_async_copy(encoder_hbm.at[:, span], table.at[:, span], sems.at[0, number]),
                pltpu.make_async_copy(wanted, held.at[span], sems.at[1, number]),
            )
        )

    def multiply(number):
        if number == 0:
            for copy in first_copies:
                copy.wait()
        span = slice(number * block, (number + 1) * block)
        scaled = (table[:, span].astype(jnp.float32) * scale_ref[:, span]).astype(jnp.bfloat16)
        return mm(scaled, held[span, :])

    add_up(4, loads, multiply, acc_ref)
    own = [comp_ref[number, pl.ds(lax.axis_index("col"), 1), :] for number in range(comp_ref.shape[0])]
    own += [exp_ref[number, pl.ds(lax.axis_index("row"), 1), :] for number in range(exp_ref.shape[0] - 1)]
    gains = [half for gain in own for half in (gain[:, :LANES], gain[:, LANES:])]
    pad = -(-len(gains) // 8) * 8
    gains += [jnp.zeros((1, LANES), jnp.float32)] * (pad - len(gains))
    gains = jnp.concatenate(gains, axis=0)
    parts, rows, _ = out_ref.shape
    width = (rows - pad) // 2
    turned = acc_ref[...].T.reshape(parts, width, 2 * LANES)
    gains = jnp.broadcast_to(gains[None], (parts, pad, LANES))
    joined = jnp.concatenate([turned[:, :, :LANES], turned[:, :, LANES:], gains], axis=1)
    out_ref[...] = joined.astype(jnp.bfloat16)
    copy = pltpu.make_async_copy(out_ref, out_hbm, small.at[len(pairs)])
    copy.start()
    copy.wait()


def encode(sources, enc_scale, encoder, comp_gain, exp_gain, parts, first):
    points, width = sources.shape
    width -= first
    skeleton = encoder.shape[0]
    pad = gain_rows(comp_gain, exp_gain)
    packed = (parts, 2 * (width // parts) + pad, LANES)
    blocks = 8
    return pl.pallas_call(
        functools.partial(encode_kernel, blocks, first),
        in_specs=[HBM] * 5,
        out_specs=HBM,
        compiler_params=pltpu.CompilerParams(vmem_limit_bytes=20 * 2**20),
        out_shape=pltpu.HBM(packed, jnp.bfloat16),
        scratch_shapes=[
            pltpu.VMEM((points, width), jnp.bfloat16),
            pltpu.VMEM((skeleton, points), jnp.bfloat16),
            pltpu.VMEM((skeleton, width), jnp.float32),
            pltpu.SemaphoreType.DMA((2, blocks)),
            pltpu.VMEM((1, points), jnp.float32),
            pltpu.VMEM(comp_gain.shape, jnp.float32),
            pltpu.VMEM(exp_gain.shape, jnp.float32),
            pltpu.VMEM(packed, jnp.bfloat16),
            pltpu.SemaphoreType.DMA((4,)),
        ],
    )(sources, in_hbm(enc_scale.reshape(1, points)), encoder, in_hbm(comp_gain), in_hbm(exp_gain))


def side_encode_kernel(blocks, sources_hbm, scale_hbm, encoder_hbm, out_ref, held, table, acc_ref, sems, scale_ref, small):
    first_copy = pltpu.make_async_copy(scale_hbm, scale_ref, small)
    first_copy.start()
    block = held.shape[0] // blocks
    loads = []
    for number in range(blocks):
        span = pl.ds(number * block, block)
        wanted = sources_hbm.at[span, pl.ds(0, held.shape[1])]
        loads.append(
            (
                pltpu.make_async_copy(encoder_hbm.at[:, span], table.at[:, span], sems.at[0, number]),
                pltpu.make_async_copy(wanted, held.at[span], sems.at[1, number]),
            )
        )

    def multiply(number):
        if number == 0:
            first_copy.wait()
        span = slice(number * block, (number + 1) * block)
        scaled = (table[:, span].astype(jnp.float32) * scale_ref[:, span]).astype(jnp.bfloat16)
        return mm(scaled, held[span, :])

    add_up(3, loads, multiply, acc_ref)
    out_ref[...] = acc_ref[...].astype(jnp.bfloat16)


def side_encode(sources, enc_scale, encoder, width):
    points = sources.shape[0]
    skeleton = encoder.shape[0]
    blocks = 4
    return pl.pallas_call(
        functools.partial(side_encode_kernel, blocks),
        in_specs=[HBM] * 3,
        out_specs=VMEM,
        compiler_params=pltpu.CompilerParams(vmem_limit_bytes=12 * 2**20),
        out_shape=jax.ShapeDtypeStruct((skeleton, width), jnp.bfloat16),
        scratch_shapes=[
            pltpu.VMEM((points, width), jnp.bfloat16),
            pltpu.VMEM((skeleton, points), jnp.bfloat16),
            pltpu.VMEM((skeleton, width), jnp.float32),
            pltpu.SemaphoreType.DMA((2, blocks)),
            pltpu.VMEM((1, points), jnp.float32),
            pltpu.SemaphoreType.DMA,
        ],
    )(sources, in_hbm(enc_scale.reshape(1, points)), encoder)


def pick_kernel(exp_hbm, *refs):
    *outs, sems = refs
    copies = []
    for number, out_ref in enumerate(outs):
        skeleton = out_ref.shape[0]
        here = pl.multiple_of(lax.axis_index("row") // 2**number % 2 * skeleton, skeleton)
        copies.append(pltpu.make_async_copy(exp_hbm.at[number, pl.ds(here, skeleton)], out_ref, sems.at[number]))
        copies[-1].start()
    for copy in copies:
        copy.wait()


def pick(exp_transfer):
    count = exp_transfer.shape[0]
    skeleton = exp_transfer.shape[1] // 2
    return pl.pallas_call(
        pick_kernel,
        in_specs=[HBM],
        out_specs=[VMEM] * count,
        compiler_params=pltpu.CompilerParams(vmem_limit_bytes=4 * 2**20),
        out_shape=[jax.ShapeDtypeStruct((skeleton, 2 * skeleton), jnp.bfloat16)] * count,
        scratch_shapes=[pltpu.SemaphoreType.DMA((count,))],
    )(in_hbm(exp_transfer))


def side_level_kernel(axis, bit, scaled, own_ref, partner_ref, rows_ref, gain_ref, out_ref):
    skeleton = own_ref.shape[0]
    position = lax.axis_index(axis)
    upper = position // 2**bit % 2
    here = pl.multiple_of(upper * skeleton, skeleton)
    there = pl.multiple_of((1 - upper) * skeleton, skeleton)
    if len(rows_ref.shape) == 3:
        rows_ref = rows_ref.at[bit, pl.ds(here, skeleton)]
    mixed = mm(rows_ref[:, pl.ds(here, skeleton)], own_ref[...])
    mixed += mm(rows_ref[:, pl.ds(there, skeleton)], partner_ref[...])
    if scaled:
        gain = jnp.broadcast_to(gain_ref[bit, pl.ds(position, 1), :], (8, skeleton)).T
        mixed *= gain[:, :1]
    out_ref[...] = mixed.astype(jnp.bfloat16)


def side_level(own, axis, bit, scaled, rows, gain):
    pairs = [(source, source ^ 2**bit) for source in range(lax.axis_size(axis))]
    partner = lax.ppermute(own, axis, pairs)
    return pl.pallas_call(
        functools.partial(side_level_kernel, axis, bit, scaled),
        in_specs=[VMEM] * 4,
        compiler_params=pltpu.CompilerParams(vmem_limit_bytes=4 * 2**20),
        out_specs=VMEM,
        out_shape=jax.ShapeDtypeStruct(own.shape, jnp.bfloat16),
    )(on_chip(own), on_chip(partner), on_chip(rows), gain)


def gain_rows(comp_gain, exp_gain):
    sent = 2 * (comp_gain.shape[0] + exp_gain.shape[0] - 1)
    return -(-sent // 8) * 8


def levels_kernel(strides, pad, packed_ref, comp_ref, exp_ref, out_ref):
    boxes, rows, _ = packed_ref.shape
    width = (rows - pad) // 2
    skeleton = 2 * LANES
    packed = packed_ref[...].astype(jnp.float32)
    state = jnp.concatenate([packed[:, :width, :], packed[:, width : 2 * width, :]], axis=-1)
    gains = packed[:, 2 * width :, :]
    for number, stride in enumerate(strides):
        turned = number >= comp_ref.shape[0]
        transfer = exp_ref[number - comp_ref.shape[0]] if turned else comp_ref[number]
        halves = state.reshape(boxes // (2 * stride), 2, stride * width, skeleton)
        low = halves[:, 0].reshape(boxes // 2 * width, skeleton).astype(jnp.bfloat16)
        high = halves[:, 1].reshape(boxes // 2 * width, skeleton).astype(jnp.bfloat16)
        mixed = mm(low, transfer[:, :skeleton], NT) + mm(high, transfer[:, skeleton:], NT)
        shape = (boxes // (2 * stride), 1, stride, width, skeleton)
        state = jnp.concatenate(
            [mixed[:, :skeleton].reshape(shape), mixed[:, skeleton:].reshape(shape)], axis=1
        ).reshape(boxes, width, skeleton)
        if number + 1 < len(strides):
            gain = jnp.concatenate(
                [gains[:, 2 * number : 2 * number + 1, :], gains[:, 2 * number + 1 : 2 * number + 2, :]],
                axis=-1,
            )
            state = state * gain
    out_ref[...] = jnp.concatenate([state[:, :, :LANES], state[:, :, LANES:]], axis=1).astype(jnp.bfloat16)


def levels(packed, comp_transfer, exp_transfer, strides, pad):
    boxes, rows, _ = packed.shape
    return pl.pallas_call(
        functools.partial(levels_kernel, strides, pad),
        in_specs=[VMEM] * 3,
        compiler_params=pltpu.CompilerParams(vmem_limit_bytes=20 * 2**20),
        out_specs=VMEM,
        out_shape=jax.ShapeDtypeStruct((boxes, rows - pad, LANES), jnp.bfloat16),
    )(on_chip(packed), on_chip(comp_transfer), on_chip(exp_transfer))


def decode_kernel(blocks, side_ref, packed_ref, decoder_ref, out_hbm, turned_ref, held, sems):
    boxes, rows, _ = packed_ref.shape
    width, side = rows // 2, side_ref.shape[1]
    packed = packed_ref[...].astype(jnp.float32)
    coeffs = jnp.concatenate([packed[:, :width, :], packed[:, width:, :]], axis=-1)
    coeffs = coeffs.reshape(boxes * width, 2 * LANES)
    turned_ref[:, :side] = side_ref[...]
    turned_ref[:, side:] = coeffs.T.astype(jnp.bfloat16)
    block = decoder_ref.shape[0] // blocks
    copies = []
    for number in range(blocks):
        span = pl.ds(number * block, block)
        rows_of = slice(number * block, (number + 1) * block)
        held[rows_of, :] = mm(decoder_ref[rows_of, :], turned_ref[...]).astype(jnp.bfloat16)
        copies.append(pltpu.make_async_copy(held.at[span], out_hbm.at[span], sems.at[number]))
        copies[-1].start()
    for copy in copies:
        copy.wait()


def decode(side, packed, decoder):
    boxes, rows, _ = packed.shape
    points, skeleton = decoder.shape
    width = side.shape[1] + boxes * rows // 2
    blocks = 8
    return pl.pallas_call(
        functools.partial(decode_kernel, blocks),
        in_specs=[VMEM, VMEM, VMEM],
        compiler_params=pltpu.CompilerParams(vmem_limit_bytes=20 * 2**20),
        out_specs=HBM,
        out_shape=jax.ShapeDtypeStruct((points, width), jnp.bfloat16),
        scratch_shapes=[
            pltpu.VMEM((skeleton, width), jnp.bfloat16),
            pltpu.VMEM((points, width), jnp.bfloat16),
            pltpu.SemaphoreType.DMA((blocks,)),
        ],
    )(on_chip(side), on_chip(packed), decoder)


def plain_encode(sources, enc_scale, encoder, comp_gain, exp_gain, parts):
    own_comp = lax.dynamic_index_in_dim(comp_gain, lax.axis_index("col"), 1, keepdims=False)
    own_exp = lax.dynamic_index_in_dim(exp_gain, lax.axis_index("row"), 1, keepdims=False)
    gains = jnp.concatenate([own_comp, own_exp[:-1]], axis=0).astype(jnp.bfloat16).reshape(-1, LANES)
    gains = jnp.pad(gains, ((0, gain_rows(comp_gain, exp_gain) - gains.shape[0]), (0, 0)))
    scaled = (encoder.astype(jnp.float32) * enc_scale[None, :]).astype(jnp.bfloat16)
    coeffs = mm(sources, scaled, (((0,), (1,)), ((), ()))).astype(jnp.bfloat16)
    coeffs = coeffs.reshape(parts, -1, 2, LANES).swapaxes(1, 2).reshape(parts, -1, LANES)
    gains = jnp.broadcast_to(gains[None], (parts, *gains.shape))
    return jnp.concatenate([coeffs, gains], axis=1)


def plain_levels(packed, comp_transfer, exp_transfer, strides, pad):
    boxes, rows, _ = packed.shape
    width = (rows - pad) // 2
    skeleton = 2 * LANES
    state = packed[:, : 2 * width].reshape(boxes, 2, width, LANES).swapaxes(1, 2).reshape(boxes, width, skeleton)
    gains = packed[:, 2 * width :].astype(jnp.float32).reshape(boxes, pad // 2, 1, skeleton)
    transfers = jnp.concatenate([comp_transfer, exp_transfer], axis=0)
    for number, stride in enumerate(strides):
        halves = state.reshape(boxes // (2 * stride), 2, stride, width, skeleton)
        stacked = jnp.concatenate([halves[:, 0], halves[:, 1]], axis=-1)
        paired = transfers[number].reshape(2, skeleton, 2 * skeleton)
        both = jnp.einsum("hlsk,tjk->htlsj", stacked, paired, preferred_element_type=jnp.float32)
        both = both.reshape(boxes, width, skeleton)
        if number + 1 < len(strides):
            both = both * gains[:, number]
        state = both.astype(jnp.bfloat16)
    return state.reshape(boxes, width, 2, LANES).swapaxes(1, 2).reshape(boxes, 2 * width, LANES)


def plain_decode(packed, decoder):
    boxes, rows, _ = packed.shape
    width = rows // 2
    coeffs = packed.reshape(boxes, 2, width, LANES).swapaxes(1, 2).reshape(boxes * width, 2 * LANES)
    return mm(decoder, coeffs, NT).astype(jnp.bfloat16)


def body(
    sources,
    enc_scale,
    encoder,
    comp_transfer,
    comp_gain,
    exp_transfer,
    exp_gain,
    decoder,
    dec_scale,
):
    col_count, row_count = lax.axis_size("col"), lax.axis_size("row")
    parts = col_count * row_count
    skeleton = encoder.shape[0]
    comp_levels, exp_levels = comp_transfer.shape[0], exp_transfer.shape[0]
    strides = tuple(2**number for number in range(comp_levels))
    strides += tuple(col_count * 2**number for number in range(exp_levels))
    comp_gain, exp_gain = comp_gain[:, 0], exp_gain[:, 0]
    pad = gain_rows(comp_gain, exp_gain)
    last_gain = lax.dynamic_index_in_dim(exp_gain[-1], lax.axis_index("row"), 0, keepdims=False)
    factors = dec_scale[:, None] * last_gain[None, :]
    width = sources.shape[1]
    side = width // 4

    if side % LANES or (width - side) % (8 * parts) or skeleton != 2 * LANES:
        packed = plain_encode(sources, enc_scale, encoder, comp_gain, exp_gain, parts)
        packed = lax.all_to_all(packed, ORDER, 0, 0, tiled=True)
        packed = plain_levels(packed, comp_transfer, exp_transfer, strides, pad)
        packed = lax.all_to_all(packed, ORDER, 0, 0, tiled=True)
        return plain_decode(packed, (decoder.astype(jnp.float32) * factors).astype(jnp.bfloat16))

    sources, encoder = in_hbm(sources), in_hbm(encoder)
    packed = encode(sources, enc_scale, encoder, comp_gain, exp_gain, parts, side)
    packed = lax.all_to_all(packed, ORDER, 0, 0, tiled=True)
    coeffs = side_encode(sources, enc_scale, encoder, side)
    rows = pick(exp_transfer)
    for number in range(comp_levels):
        coeffs = side_level(coeffs, "col", number, True, comp_transfer, comp_gain)
    packed = levels(packed, comp_transfer, exp_transfer, strides, pad)
    packed = lax.all_to_all(packed, ORDER, 0, 0, tiled=True)
    for number in range(exp_levels):
        coeffs = side_level(coeffs, "row", number, number + 1 < exp_levels, rows[number], exp_gain)
    table = on_chip((decoder.astype(jnp.float32) * factors).astype(jnp.bfloat16))
    return decode(coeffs, packed, table)


def solution(mesh):
    in_specs = (
        P(AXES, None),
        P(AXES),
        P(),
        P(),
        P(None, "row", None, None),
        P(),
        P(None, "col", None, None),
        P(),
        P(AXES),
    )

    def step(*args):
        return jax.shard_map(body, mesh=mesh, in_specs=in_specs, out_specs=P(AXES, None), check_vma=False)(*args)

    return step
```

```python
import functools

import jax
import jax.numpy as jnp
from jax import lax
from jax.experimental import pallas as pl
from jax.experimental.pallas import tpu as pltpu
from jax.sharding import PartitionSpec as P


AXES = ("col", "row")
ORDER = ("row", "col")
LANES = 128
NT = (((1,), (1,)), ((), ()))
HBM = pl.BlockSpec(memory_space=pltpu.HBM)
VMEM = pl.BlockSpec(memory_space=pltpu.VMEM)


def on_chip(value):
    return pltpu.with_memory_space_constraint(value, pltpu.VMEM)


def in_hbm(value):
    return pltpu.with_memory_space_constraint(value, pltpu.HBM)


def mm(a, b, dims=(((1,), (0,)), ((), ()))):
    return lax.dot_general(a, b, dims, preferred_element_type=jnp.float32)


def add_up(window, loads, multiply, acc_ref):
    for copies in loads[:window]:
        for copy in copies:
            copy.start()
    for number, copies in enumerate(loads):
        for copy in copies:
            copy.wait()
        for copy in loads[number + window] if number + window < len(loads) else ():
            copy.start()
        if number == 0:
            acc_ref[...] = multiply(number)
        else:
            acc_ref[...] += multiply(number)


def encode_kernel(
    blocks,
    first,
    sources_hbm,
    scale_hbm,
    encoder_hbm,
    comp_hbm,
    exp_hbm,
    out_hbm,
    held,
    table,
    acc_ref,
    sems,
    scale_ref,
    comp_ref,
    exp_ref,
    out_ref,
    small,
):
    pairs = ((scale_hbm, scale_ref), (comp_hbm, comp_ref), (exp_hbm, exp_ref))
    first_copies = [pltpu.make_async_copy(*pair, small.at[number]) for number, pair in enumerate(pairs)]
    for copy in first_copies:
        copy.start()
    block = held.shape[0] // blocks
    loads = []
    for number in range(blocks):
        span = pl.ds(number * block, block)
        wanted = sources_hbm.at[span, pl.ds(first, held.shape[1])]
        loads.append(
            (
                pltpu.make_async_copy(encoder_hbm.at[:, span], table.at[:, span], sems.at[0, number]),
                pltpu.make_async_copy(wanted, held.at[span], sems.at[1, number]),
            )
        )

    def multiply(number):
        if number == 0:
            for copy in first_copies:
                copy.wait()
        span = slice(number * block, (number + 1) * block)
        scaled = (table[:, span].astype(jnp.float32) * scale_ref[:, span]).astype(jnp.bfloat16)
        return mm(scaled, held[span, :])

    add_up(4, loads, multiply, acc_ref)
    own = [comp_ref[number, pl.ds(lax.axis_index("col"), 1), :] for number in range(comp_ref.shape[0])]
    own += [exp_ref[number, pl.ds(lax.axis_index("row"), 1), :] for number in range(exp_ref.shape[0] - 1)]
    gains = [half for gain in own for half in (gain[:, :LANES], gain[:, LANES:])]
    pad = -(-len(gains) // 8) * 8
    gains += [jnp.zeros((1, LANES), jnp.float32)] * (pad - len(gains))
    gains = jnp.concatenate(gains, axis=0)
    parts, rows, _ = out_ref.shape
    width = (rows - pad) // 2
    groups = 2
    some = parts // groups
    gains = jnp.broadcast_to(gains[None], (some, pad, LANES))
    copies = []
    for number in range(groups):
        turned = acc_ref[:, number * some * width : (number + 1) * some * width].T.reshape(some, width, 2 * LANES)
        joined = jnp.concatenate([turned[:, :, :LANES], turned[:, :, LANES:], gains], axis=1)
        out_ref[number * some : (number + 1) * some] = joined.astype(jnp.bfloat16)
        span = pl.ds(number * some, some)
        copies.append(pltpu.make_async_copy(out_ref.at[span], out_hbm.at[span], small.at[len(pairs) + number]))
        copies[-1].start()
    for copy in copies:
        copy.wait()


def encode(sources, enc_scale, encoder, comp_gain, exp_gain, parts, first):
    points, width = sources.shape
    width -= first
    skeleton = encoder.shape[0]
    pad = gain_rows(comp_gain, exp_gain)
    packed = (parts, 2 * (width // parts) + pad, LANES)
    blocks = 8
    return pl.pallas_call(
        functools.partial(encode_kernel, blocks, first),
        in_specs=[HBM] * 5,
        out_specs=HBM,
        compiler_params=pltpu.CompilerParams(vmem_limit_bytes=20 * 2**20),
        out_shape=pltpu.HBM(packed, jnp.bfloat16),
        scratch_shapes=[
            pltpu.VMEM((points, width), jnp.bfloat16),
            pltpu.VMEM((skeleton, points), jnp.bfloat16),
            pltpu.VMEM((skeleton, width), jnp.float32),
            pltpu.SemaphoreType.DMA((2, blocks)),
            pltpu.VMEM((1, points), jnp.float32),
            pltpu.VMEM(comp_gain.shape, jnp.float32),
            pltpu.VMEM(exp_gain.shape, jnp.float32),
            pltpu.VMEM(packed, jnp.bfloat16),
            pltpu.SemaphoreType.DMA((5,)),
        ],
    )(sources, in_hbm(enc_scale.reshape(1, points)), encoder, in_hbm(comp_gain), in_hbm(exp_gain))


def side_encode_kernel(blocks, sources_hbm, scale_hbm, encoder_hbm, out_ref, held, table, acc_ref, sems, scale_ref, small):
    first_copy = pltpu.make_async_copy(scale_hbm, scale_ref, small)
    first_copy.start()
    block = held.shape[0] // blocks
    loads = []
    for number in range(blocks):
        span = pl.ds(number * block, block)
        wanted = sources_hbm.at[span, pl.ds(0, held.shape[1])]
        loads.append(
            (
                pltpu.make_async_copy(encoder_hbm.at[:, span], table.at[:, span], sems.at[0, number]),
                pltpu.make_async_copy(wanted, held.at[span], sems.at[1, number]),
            )
        )

    def multiply(number):
        if number == 0:
            first_copy.wait()
        span = slice(number * block, (number + 1) * block)
        scaled = (table[:, span].astype(jnp.float32) * scale_ref[:, span]).astype(jnp.bfloat16)
        return mm(scaled, held[span, :])

    add_up(3, loads, multiply, acc_ref)
    out_ref[...] = acc_ref[...].astype(jnp.bfloat16)


def side_encode(sources, enc_scale, encoder, width):
    points = sources.shape[0]
    skeleton = encoder.shape[0]
    blocks = 4
    return pl.pallas_call(
        functools.partial(side_encode_kernel, blocks),
        in_specs=[HBM] * 3,
        out_specs=VMEM,
        compiler_params=pltpu.CompilerParams(vmem_limit_bytes=12 * 2**20),
        out_shape=jax.ShapeDtypeStruct((skeleton, width), jnp.bfloat16),
        scratch_shapes=[
            pltpu.VMEM((points, width), jnp.bfloat16),
            pltpu.VMEM((skeleton, points), jnp.bfloat16),
            pltpu.VMEM((skeleton, width), jnp.float32),
            pltpu.SemaphoreType.DMA((2, blocks)),
            pltpu.VMEM((1, points), jnp.float32),
            pltpu.SemaphoreType.DMA,
        ],
    )(sources, in_hbm(enc_scale.reshape(1, points)), encoder)


def pick_kernel(exp_hbm, *refs):
    *outs, sems = refs
    copies = []
    for number, out_ref in enumerate(outs):
        skeleton = out_ref.shape[0]
        here = pl.multiple_of(lax.axis_index("row") // 2**number % 2 * skeleton, skeleton)
        copies.append(pltpu.make_async_copy(exp_hbm.at[number, pl.ds(here, skeleton)], out_ref, sems.at[number]))
        copies[-1].start()
    for copy in copies:
        copy.wait()


def pick(exp_transfer):
    count = exp_transfer.shape[0]
    skeleton = exp_transfer.shape[1] // 2
    return pl.pallas_call(
        pick_kernel,
        in_specs=[HBM],
        out_specs=[VMEM] * count,
        compiler_params=pltpu.CompilerParams(vmem_limit_bytes=4 * 2**20),
        out_shape=[jax.ShapeDtypeStruct((skeleton, 2 * skeleton), jnp.bfloat16)] * count,
        scratch_shapes=[pltpu.SemaphoreType.DMA((count,))],
    )(in_hbm(exp_transfer))


def mix(axis, bit, own_ref, partner_ref, rows_ref):
    skeleton = own_ref.shape[0]
    upper = lax.axis_index(axis) // 2**bit % 2
    here = pl.multiple_of(upper * skeleton, skeleton)
    there = pl.multiple_of((1 - upper) * skeleton, skeleton)
    if len(rows_ref.shape) == 3:
        rows_ref = rows_ref.at[bit, pl.ds(here, skeleton)]
    mixed = mm(rows_ref[:, pl.ds(here, skeleton)], own_ref[...])
    return mixed + mm(rows_ref[:, pl.ds(there, skeleton)], partner_ref[...])


def side_level_kernel(axis, bit, own_ref, partner_ref, rows_ref, gain_ref, out_ref):
    mixed = mix(axis, bit, own_ref, partner_ref, rows_ref)
    gain = gain_ref[bit, pl.ds(lax.axis_index(axis), 1), :]
    mixed *= jnp.broadcast_to(gain, (8, gain.shape[1])).T[:, :1]
    out_ref[...] = mixed.astype(jnp.bfloat16)


def from_partner(own, axis, bit):
    return lax.ppermute(own, axis, [(source, source ^ 2**bit) for source in range(lax.axis_size(axis))])


def side_level(own, axis, bit, rows, gain):
    partner = from_partner(own, axis, bit)
    return pl.pallas_call(
        functools.partial(side_level_kernel, axis, bit),
        in_specs=[VMEM] * 4,
        compiler_params=pltpu.CompilerParams(vmem_limit_bytes=4 * 2**20),
        out_specs=VMEM,
        out_shape=jax.ShapeDtypeStruct(own.shape, jnp.bfloat16),
    )(on_chip(own), on_chip(partner), on_chip(rows), gain)


def gain_rows(comp_gain, exp_gain):
    sent = 2 * (comp_gain.shape[0] + exp_gain.shape[0] - 1)
    return -(-sent // 8) * 8


def levels_kernel(strides, pad, packed_ref, comp_ref, exp_ref, out_ref):
    boxes, rows, _ = packed_ref.shape
    width = (rows - pad) // 2
    skeleton = 2 * LANES
    packed = packed_ref[...].astype(jnp.float32)
    state = jnp.concatenate([packed[:, :width, :], packed[:, width : 2 * width, :]], axis=-1)
    gains = packed[:, 2 * width :, :]
    for number, stride in enumerate(strides):
        turned = number >= comp_ref.shape[0]
        transfer = exp_ref[number - comp_ref.shape[0]] if turned else comp_ref[number]
        halves = state.reshape(boxes // (2 * stride), 2, stride * width, skeleton)
        low = halves[:, 0].reshape(boxes // 2 * width, skeleton).astype(jnp.bfloat16)
        high = halves[:, 1].reshape(boxes // 2 * width, skeleton).astype(jnp.bfloat16)
        mixed = mm(low, transfer[:, :skeleton], NT) + mm(high, transfer[:, skeleton:], NT)
        shape = (boxes // (2 * stride), 1, stride, width, skeleton)
        state = jnp.concatenate(
            [mixed[:, :skeleton].reshape(shape), mixed[:, skeleton:].reshape(shape)], axis=1
        ).reshape(boxes, width, skeleton)
        if number + 1 < len(strides):
            gain = jnp.concatenate(
                [gains[:, 2 * number : 2 * number + 1, :], gains[:, 2 * number + 1 : 2 * number + 2, :]],
                axis=-1,
            )
            state = state * gain
    out_ref[...] = jnp.concatenate([state[:, :, :LANES], state[:, :, LANES:]], axis=1).astype(jnp.bfloat16)


def levels(packed, comp_transfer, exp_transfer, strides, pad):
    boxes, rows, _ = packed.shape
    return pl.pallas_call(
        functools.partial(levels_kernel, strides, pad),
        in_specs=[VMEM] * 3,
        compiler_params=pltpu.CompilerParams(vmem_limit_bytes=20 * 2**20),
        out_specs=VMEM,
        out_shape=jax.ShapeDtypeStruct((boxes, rows - pad, LANES), jnp.bfloat16),
    )(on_chip(packed), on_chip(comp_transfer), on_chip(exp_transfer))


def decode_kernel(blocks, bit, side_ref, partner_ref, rows_ref, packed_ref, decoder_ref, out_hbm, turned_ref, held, sems):
    boxes, rows, _ = packed_ref.shape
    width, side = rows // 2, side_ref.shape[1]
    packed = packed_ref[...].astype(jnp.float32)
    coeffs = jnp.concatenate([packed[:, :width, :], packed[:, width:, :]], axis=-1)
    coeffs = coeffs.reshape(boxes * width, 2 * LANES)
    turned_ref[:, :side] = mix("row", bit, side_ref, partner_ref, rows_ref).astype(jnp.bfloat16)
    turned_ref[:, side:] = coeffs.T.astype(jnp.bfloat16)
    block = decoder_ref.shape[0] // blocks
    copies = []
    for number in range(blocks):
        span = pl.ds(number * block, block)
        rows_of = slice(number * block, (number + 1) * block)
        held[rows_of, :] = mm(decoder_ref[rows_of, :], turned_ref[...]).astype(jnp.bfloat16)
        copies.append(pltpu.make_async_copy(held.at[span], out_hbm.at[span], sems.at[number]))
        copies[-1].start()
    for copy in copies:
        copy.wait()


def decode(bit, side, partner, last_rows, packed, decoder):
    boxes, rows, _ = packed.shape
    points, skeleton = decoder.shape
    width = side.shape[1] + boxes * rows // 2
    blocks = 8
    return pl.pallas_call(
        functools.partial(decode_kernel, blocks, bit),
        in_specs=[VMEM] * 5,
        compiler_params=pltpu.CompilerParams(vmem_limit_bytes=20 * 2**20),
        out_specs=HBM,
        out_shape=jax.ShapeDtypeStruct((points, width), jnp.bfloat16),
        scratch_shapes=[
            pltpu.VMEM((skeleton, width), jnp.bfloat16),
            pltpu.VMEM((points, width), jnp.bfloat16),
            pltpu.SemaphoreType.DMA((blocks,)),
        ],
    )(on_chip(side), on_chip(partner), on_chip(last_rows), on_chip(packed), decoder)


def plain_encode(sources, enc_scale, encoder, comp_gain, exp_gain, parts):
    own_comp = lax.dynamic_index_in_dim(comp_gain, lax.axis_index("col"), 1, keepdims=False)
    own_exp = lax.dynamic_index_in_dim(exp_gain, lax.axis_index("row"), 1, keepdims=False)
    gains = jnp.concatenate([own_comp, own_exp[:-1]], axis=0).astype(jnp.bfloat16).reshape(-1, LANES)
    gains = jnp.pad(gains, ((0, gain_rows(comp_gain, exp_gain) - gains.shape[0]), (0, 0)))
    scaled = (encoder.astype(jnp.float32) * enc_scale[None, :]).astype(jnp.bfloat16)
    coeffs = mm(sources, scaled, (((0,), (1,)), ((), ()))).astype(jnp.bfloat16)
    coeffs = coeffs.reshape(parts, -1, 2, LANES).swapaxes(1, 2).reshape(parts, -1, LANES)
    gains = jnp.broadcast_to(gains[None], (parts, *gains.shape))
    return jnp.concatenate([coeffs, gains], axis=1)


def plain_levels(packed, comp_transfer, exp_transfer, strides, pad):
    boxes, rows, _ = packed.shape
    width = (rows - pad) // 2
    skeleton = 2 * LANES
    state = packed[:, : 2 * width].reshape(boxes, 2, width, LANES).swapaxes(1, 2).reshape(boxes, width, skeleton)
    gains = packed[:, 2 * width :].astype(jnp.float32).reshape(boxes, pad // 2, 1, skeleton)
    transfers = jnp.concatenate([comp_transfer, exp_transfer], axis=0)
    for number, stride in enumerate(strides):
        halves = state.reshape(boxes // (2 * stride), 2, stride, width, skeleton)
        stacked = jnp.concatenate([halves[:, 0], halves[:, 1]], axis=-1)
        paired = transfers[number].reshape(2, skeleton, 2 * skeleton)
        both = jnp.einsum("hlsk,tjk->htlsj", stacked, paired, preferred_element_type=jnp.float32)
        both = both.reshape(boxes, width, skeleton)
        if number + 1 < len(strides):
            both = both * gains[:, number]
        state = both.astype(jnp.bfloat16)
    return state.reshape(boxes, width, 2, LANES).swapaxes(1, 2).reshape(boxes, 2 * width, LANES)


def plain_decode(packed, decoder):
    boxes, rows, _ = packed.shape
    width = rows // 2
    coeffs = packed.reshape(boxes, 2, width, LANES).swapaxes(1, 2).reshape(boxes * width, 2 * LANES)
    return mm(decoder, coeffs, NT).astype(jnp.bfloat16)


def body(
    sources,
    enc_scale,
    encoder,
    comp_transfer,
    comp_gain,
    exp_transfer,
    exp_gain,
    decoder,
    dec_scale,
):
    col_count, row_count = lax.axis_size("col"), lax.axis_size("row")
    parts = col_count * row_count
    skeleton = encoder.shape[0]
    comp_levels, exp_levels = comp_transfer.shape[0], exp_transfer.shape[0]
    strides = tuple(2**number for number in range(comp_levels))
    strides += tuple(col_count * 2**number for number in range(exp_levels))
    comp_gain, exp_gain = comp_gain[:, 0], exp_gain[:, 0]
    pad = gain_rows(comp_gain, exp_gain)
    last_gain = lax.dynamic_index_in_dim(exp_gain[-1], lax.axis_index("row"), 0, keepdims=False)
    factors = dec_scale[:, None] * last_gain[None, :]
    width = sources.shape[1]
    side = width // 4

    if side % LANES or (width - side) % (8 * parts) or skeleton != 2 * LANES:
        packed = plain_encode(sources, enc_scale, encoder, comp_gain, exp_gain, parts)
        packed = lax.all_to_all(packed, ORDER, 0, 0, tiled=True)
        packed = plain_levels(packed, comp_transfer, exp_transfer, strides, pad)
        packed = lax.all_to_all(packed, ORDER, 0, 0, tiled=True)
        return plain_decode(packed, (decoder.astype(jnp.float32) * factors).astype(jnp.bfloat16))

    sources, encoder = in_hbm(sources), in_hbm(encoder)
    packed = encode(sources, enc_scale, encoder, comp_gain, exp_gain, parts, side)
    packed = lax.all_to_all(packed, ORDER, 0, 0, tiled=True)
    coeffs = side_encode(sources, enc_scale, encoder, side)
    rows = pick(exp_transfer)
    for number in range(comp_levels):
        coeffs = side_level(coeffs, "col", number, comp_transfer, comp_gain)
    packed = levels(packed, comp_transfer, exp_transfer, strides, pad)
    packed = lax.all_to_all(packed, ORDER, 0, 0, tiled=True)
    for number in range(exp_levels - 1):
        coeffs = side_level(coeffs, "row", number, rows[number], exp_gain)
    partner = from_partner(coeffs, "row", exp_levels - 1)
    table = on_chip((decoder.astype(jnp.float32) * factors).astype(jnp.bfloat16))
    return decode(exp_levels - 1, coeffs, partner, rows[exp_levels - 1], packed, table)


def solution(mesh):
    in_specs = (
        P(AXES, None),
        P(AXES),
        P(),
        P(),
        P(None, "row", None, None),
        P(),
        P(None, "col", None, None),
        P(),
        P(AXES),
    )

    def step(*args):
        return jax.shard_map(body, mesh=mesh, in_specs=in_specs, out_specs=P(AXES, None), check_vma=False)(*args)

    return step
```

```python
import functools

import jax
import jax.numpy as jnp
from jax import lax
from jax.experimental import pallas as pl
from jax.experimental.pallas import tpu as pltpu
from jax.sharding import PartitionSpec as P


AXES = ("col", "row")
ORDER = ("row", "col")
LANES = 128
NT = (((1,), (1,)), ((), ()))
HBM = pl.BlockSpec(memory_space=pltpu.HBM)
VMEM = pl.BlockSpec(memory_space=pltpu.VMEM)


def on_chip(value):
    return pltpu.with_memory_space_constraint(value, pltpu.VMEM)


def in_hbm(value):
    return pltpu.with_memory_space_constraint(value, pltpu.HBM)


def mm(a, b, dims=(((1,), (0,)), ((), ()))):
    return lax.dot_general(a, b, dims, preferred_element_type=jnp.float32)


def add_up(window, loads, multiply, acc_ref):
    for copies in loads[:window]:
        for copy in copies:
            copy.start()
    for number, copies in enumerate(loads):
        for copy in copies:
            copy.wait()
        for copy in loads[number + window] if number + window < len(loads) else ():
            copy.start()
        if number == 0:
            acc_ref[...] = multiply(number)
        else:
            acc_ref[...] += multiply(number)


def encode_kernel(
    blocks,
    first,
    sources_hbm,
    scale_hbm,
    encoder_hbm,
    comp_hbm,
    exp_hbm,
    out_hbm,
    held,
    table,
    acc_ref,
    sems,
    scale_ref,
    comp_ref,
    exp_ref,
    out_ref,
    small,
):
    pairs = ((scale_hbm, scale_ref), (comp_hbm, comp_ref), (exp_hbm, exp_ref))
    first_copies = [pltpu.make_async_copy(*pair, small.at[number]) for number, pair in enumerate(pairs)]
    for copy in first_copies:
        copy.start()
    block = held.shape[0] // blocks
    loads = []
    for number in range(blocks):
        span = pl.ds(number * block, block)
        wanted = sources_hbm.at[span, pl.ds(first, held.shape[1])]
        loads.append(
            (
                pltpu.make_async_copy(encoder_hbm.at[:, span], table.at[:, span], sems.at[0, number]),
                pltpu.make_async_copy(wanted, held.at[span], sems.at[1, number]),
            )
        )

    def multiply(number):
        if number == 0:
            for copy in first_copies:
                copy.wait()
        span = slice(number * block, (number + 1) * block)
        scaled = (table[:, span].astype(jnp.float32) * scale_ref[:, span]).astype(jnp.bfloat16)
        return mm(scaled, held[span, :])

    add_up(4, loads, multiply, acc_ref)
    own = [comp_ref[number, pl.ds(lax.axis_index("col"), 1), :] for number in range(comp_ref.shape[0])]
    own += [exp_ref[number, pl.ds(lax.axis_index("row"), 1), :] for number in range(exp_ref.shape[0] - 1)]
    gains = [half for gain in own for half in (gain[:, :LANES], gain[:, LANES:])]
    pad = -(-len(gains) // 8) * 8
    gains += [jnp.zeros((1, LANES), jnp.float32)] * (pad - len(gains))
    gains = jnp.concatenate(gains, axis=0)
    parts, rows, _ = out_ref.shape
    width = (rows - pad) // 2
    groups = 2
    some = parts // groups
    gains = jnp.broadcast_to(gains[None], (some, pad, LANES))
    copies = []
    for number in range(groups):
        turned = acc_ref[:, number * some * width : (number + 1) * some * width].T.reshape(some, width, 2 * LANES)
        joined = jnp.concatenate([turned[:, :, :LANES], turned[:, :, LANES:], gains], axis=1)
        out_ref[number * some : (number + 1) * some] = joined.astype(jnp.bfloat16)
        span = pl.ds(number * some, some)
        copies.append(pltpu.make_async_copy(out_ref.at[span], out_hbm.at[span], small.at[len(pairs) + number]))
        copies[-1].start()
    for copy in copies:
        copy.wait()


def encode(sources, enc_scale, encoder, comp_gain, exp_gain, parts, first):
    points, width = sources.shape
    width -= first
    skeleton = encoder.shape[0]
    pad = gain_rows(comp_gain, exp_gain)
    packed = (parts, 2 * (width // parts) + pad, LANES)
    blocks = 8
    return pl.pallas_call(
        functools.partial(encode_kernel, blocks, first),
        in_specs=[HBM] * 5,
        out_specs=HBM,
        compiler_params=pltpu.CompilerParams(vmem_limit_bytes=20 * 2**20),
        out_shape=pltpu.HBM(packed, jnp.bfloat16),
        scratch_shapes=[
            pltpu.VMEM((points, width), jnp.bfloat16),
            pltpu.VMEM((skeleton, points), jnp.bfloat16),
            pltpu.VMEM((skeleton, width), jnp.float32),
            pltpu.SemaphoreType.DMA((2, blocks)),
            pltpu.VMEM((1, points), jnp.float32),
            pltpu.VMEM(comp_gain.shape, jnp.float32),
            pltpu.VMEM(exp_gain.shape, jnp.float32),
            pltpu.VMEM(packed, jnp.bfloat16),
            pltpu.SemaphoreType.DMA((5,)),
        ],
    )(sources, in_hbm(enc_scale.reshape(1, points)), encoder, in_hbm(comp_gain), in_hbm(exp_gain))


def side_encode_kernel(blocks, sources_hbm, scale_hbm, encoder_hbm, out_ref, held, table, acc_ref, sems, scale_ref, small):
    first_copy = pltpu.make_async_copy(scale_hbm, scale_ref, small)
    first_copy.start()
    block = held.shape[0] // blocks
    loads = []
    for number in range(blocks):
        span = pl.ds(number * block, block)
        wanted = sources_hbm.at[span, pl.ds(0, held.shape[1])]
        loads.append(
            (
                pltpu.make_async_copy(encoder_hbm.at[:, span], table.at[:, span], sems.at[0, number]),
                pltpu.make_async_copy(wanted, held.at[span], sems.at[1, number]),
            )
        )

    def multiply(number):
        if number == 0:
            first_copy.wait()
        span = slice(number * block, (number + 1) * block)
        scaled = (table[:, span].astype(jnp.float32) * scale_ref[:, span]).astype(jnp.bfloat16)
        return mm(scaled, held[span, :])

    add_up(3, loads, multiply, acc_ref)
    out_ref[...] = acc_ref[...].astype(jnp.bfloat16)


def side_encode(sources, enc_scale, encoder, width):
    points = sources.shape[0]
    skeleton = encoder.shape[0]
    blocks = 4
    return pl.pallas_call(
        functools.partial(side_encode_kernel, blocks),
        in_specs=[HBM] * 3,
        out_specs=VMEM,
        compiler_params=pltpu.CompilerParams(vmem_limit_bytes=12 * 2**20),
        out_shape=jax.ShapeDtypeStruct((skeleton, width), jnp.bfloat16),
        scratch_shapes=[
            pltpu.VMEM((points, width), jnp.bfloat16),
            pltpu.VMEM((skeleton, points), jnp.bfloat16),
            pltpu.VMEM((skeleton, width), jnp.float32),
            pltpu.SemaphoreType.DMA((2, blocks)),
            pltpu.VMEM((1, points), jnp.float32),
            pltpu.SemaphoreType.DMA,
        ],
    )(sources, in_hbm(enc_scale.reshape(1, points)), encoder)


def pick_kernel(exp_hbm, *refs):
    *outs, sems = refs
    copies = []
    for number, out_ref in enumerate(outs):
        skeleton = out_ref.shape[0]
        here = pl.multiple_of(lax.axis_index("row") // 2**number % 2 * skeleton, skeleton)
        copies.append(pltpu.make_async_copy(exp_hbm.at[number, pl.ds(here, skeleton)], out_ref, sems.at[number]))
        copies[-1].start()
    for copy in copies:
        copy.wait()


def pick(exp_transfer):
    count = exp_transfer.shape[0]
    skeleton = exp_transfer.shape[1] // 2
    return pl.pallas_call(
        pick_kernel,
        in_specs=[HBM],
        out_specs=[VMEM] * count,
        compiler_params=pltpu.CompilerParams(vmem_limit_bytes=4 * 2**20),
        out_shape=[jax.ShapeDtypeStruct((skeleton, 2 * skeleton), jnp.bfloat16)] * count,
        scratch_shapes=[pltpu.SemaphoreType.DMA((count,))],
    )(in_hbm(exp_transfer))


def mix(axis, bit, own_ref, partner_ref, rows_ref):
    skeleton = own_ref.shape[0]
    upper = lax.axis_index(axis) // 2**bit % 2
    here = pl.multiple_of(upper * skeleton, skeleton)
    there = pl.multiple_of((1 - upper) * skeleton, skeleton)
    if len(rows_ref.shape) == 3:
        rows_ref = rows_ref.at[bit, pl.ds(here, skeleton)]
    mixed = mm(rows_ref[:, pl.ds(here, skeleton)], own_ref[...])
    return mixed + mm(rows_ref[:, pl.ds(there, skeleton)], partner_ref[...])


def side_level_kernel(axis, bit, own_ref, partner_ref, rows_ref, gain_ref, out_ref):
    mixed = mix(axis, bit, own_ref, partner_ref, rows_ref)
    gain = gain_ref[bit, pl.ds(lax.axis_index(axis), 1), :]
    mixed *= jnp.broadcast_to(gain, (8, gain.shape[1])).T[:, :1]
    out_ref[...] = mixed.astype(jnp.bfloat16)


def from_partner(own, axis, bit):
    return lax.ppermute(own, axis, [(source, source ^ 2**bit) for source in range(lax.axis_size(axis))])


def side_level(own, axis, bit, rows, gain):
    partner = from_partner(own, axis, bit)
    return pl.pallas_call(
        functools.partial(side_level_kernel, axis, bit),
        in_specs=[VMEM] * 4,
        compiler_params=pltpu.CompilerParams(vmem_limit_bytes=4 * 2**20),
        out_specs=VMEM,
        out_shape=jax.ShapeDtypeStruct(own.shape, jnp.bfloat16),
    )(on_chip(own), on_chip(partner), on_chip(rows), gain)


def gain_rows(comp_gain, exp_gain):
    sent = 2 * (comp_gain.shape[0] + exp_gain.shape[0] - 1)
    return -(-sent // 8) * 8


def levels_kernel(strides, pad, packed_ref, comp_ref, exp_ref, out_ref):
    boxes, rows, _ = packed_ref.shape
    width = (rows - pad) // 2
    skeleton = 2 * LANES
    packed = packed_ref[...].astype(jnp.float32)
    state = jnp.concatenate([packed[:, :width, :], packed[:, width : 2 * width, :]], axis=-1)
    gains = packed[:, 2 * width :, :]
    for number, stride in enumerate(strides):
        turned = number >= comp_ref.shape[0]
        transfer = exp_ref[number - comp_ref.shape[0]] if turned else comp_ref[number]
        halves = state.reshape(boxes // (2 * stride), 2, stride * width, skeleton)
        low = halves[:, 0].reshape(boxes // 2 * width, skeleton).astype(jnp.bfloat16)
        high = halves[:, 1].reshape(boxes // 2 * width, skeleton).astype(jnp.bfloat16)
        mixed = mm(jnp.concatenate([low, high], axis=1), transfer, NT)
        shape = (boxes // (2 * stride), 1, stride, width, skeleton)
        state = jnp.concatenate(
            [mixed[:, :skeleton].reshape(shape), mixed[:, skeleton:].reshape(shape)], axis=1
        ).reshape(boxes, width, skeleton)
        if number + 1 < len(strides):
            gain = jnp.concatenate(
                [gains[:, 2 * number : 2 * number + 1, :], gains[:, 2 * number + 1 : 2 * number + 2, :]],
                axis=-1,
            )
            state = state * gain
    out_ref[...] = jnp.concatenate([state[:, :, :LANES], state[:, :, LANES:]], axis=1).astype(jnp.bfloat16)


def levels(packed, comp_transfer, exp_transfer, strides, pad):
    boxes, rows, _ = packed.shape
    return pl.pallas_call(
        functools.partial(levels_kernel, strides, pad),
        in_specs=[VMEM] * 3,
        compiler_params=pltpu.CompilerParams(vmem_limit_bytes=20 * 2**20),
        out_specs=VMEM,
        out_shape=jax.ShapeDtypeStruct((boxes, rows - pad, LANES), jnp.bfloat16),
    )(on_chip(packed), on_chip(comp_transfer), on_chip(exp_transfer))


def put_out(first, coeffs_ref, decoder_ref, out_hbm, held, sems):
    blocks = sems.shape[0]
    block = decoder_ref.shape[0] // blocks
    copies = []
    for number in range(blocks):
        span = pl.ds(number * block, block)
        rows_of = slice(number * block, (number + 1) * block)
        held[rows_of, :] = mm(decoder_ref[rows_of, :], coeffs_ref[...]).astype(jnp.bfloat16)
        target = out_hbm.at[span, pl.ds(first, held.shape[1])]
        copies.append(pltpu.make_async_copy(held.at[span], target, sems.at[number]))
        copies[-1].start()
    for copy in copies:
        copy.wait()


def decode_kernel(first, packed_ref, decoder_ref, out_hbm, turned_ref, held, sems):
    boxes, rows, _ = packed_ref.shape
    width = rows // 2
    packed = packed_ref[...].astype(jnp.float32)
    coeffs = jnp.concatenate([packed[:, :width, :], packed[:, width:, :]], axis=-1)
    turned_ref[...] = coeffs.reshape(boxes * width, 2 * LANES).T.astype(jnp.bfloat16)
    put_out(first, turned_ref, decoder_ref, out_hbm, held, sems)


def decode(packed, decoder, first):
    boxes, rows, _ = packed.shape
    points, skeleton = decoder.shape
    width = boxes * rows // 2
    return pl.pallas_call(
        functools.partial(decode_kernel, first),
        in_specs=[VMEM, VMEM],
        compiler_params=pltpu.CompilerParams(vmem_limit_bytes=16 * 2**20),
        out_specs=HBM,
        out_shape=pltpu.HBM((points, first + width), jnp.bfloat16),
        scratch_shapes=[
            pltpu.VMEM((skeleton, width), jnp.bfloat16),
            pltpu.VMEM((points, width), jnp.bfloat16),
            pltpu.SemaphoreType.DMA((8,)),
        ],
    )(on_chip(packed), decoder)


def side_decode_kernel(bit, own_ref, partner_ref, rows_ref, decoder_ref, given_hbm, out_hbm, coeffs_ref, held, sems):
    coeffs_ref[...] = mix("row", bit, own_ref, partner_ref, rows_ref).astype(jnp.bfloat16)
    put_out(0, coeffs_ref, decoder_ref, out_hbm, held, sems)


def side_decode(bit, own, partner, rows, decoder, given):
    points = decoder.shape[0]
    return pl.pallas_call(
        functools.partial(side_decode_kernel, bit),
        in_specs=[VMEM] * 4 + [HBM],
        compiler_params=pltpu.CompilerParams(vmem_limit_bytes=8 * 2**20),
        out_specs=HBM,
        out_shape=pltpu.HBM(given.shape, jnp.bfloat16),
        scratch_shapes=[
            pltpu.VMEM(own.shape, jnp.bfloat16),
            pltpu.VMEM((points, own.shape[1]), jnp.bfloat16),
            pltpu.SemaphoreType.DMA((4,)),
        ],
        input_output_aliases={4: 0},
    )(on_chip(own), on_chip(partner), on_chip(rows), decoder, in_hbm(given))


def plain_encode(sources, enc_scale, encoder, comp_gain, exp_gain, parts):
    own_comp = lax.dynamic_index_in_dim(comp_gain, lax.axis_index("col"), 1, keepdims=False)
    own_exp = lax.dynamic_index_in_dim(exp_gain, lax.axis_index("row"), 1, keepdims=False)
    gains = jnp.concatenate([own_comp, own_exp[:-1]], axis=0).astype(jnp.bfloat16).reshape(-1, LANES)
    gains = jnp.pad(gains, ((0, gain_rows(comp_gain, exp_gain) - gains.shape[0]), (0, 0)))
    scaled = (encoder.astype(jnp.float32) * enc_scale[None, :]).astype(jnp.bfloat16)
    coeffs = mm(sources, scaled, (((0,), (1,)), ((), ()))).astype(jnp.bfloat16)
    coeffs = coeffs.reshape(parts, -1, 2, LANES).swapaxes(1, 2).reshape(parts, -1, LANES)
    gains = jnp.broadcast_to(gains[None], (parts, *gains.shape))
    return jnp.concatenate([coeffs, gains], axis=1)


def plain_levels(packed, comp_transfer, exp_transfer, strides, pad):
    boxes, rows, _ = packed.shape
    width = (rows - pad) // 2
    skeleton = 2 * LANES
    state = packed[:, : 2 * width].reshape(boxes, 2, width, LANES).swapaxes(1, 2).reshape(boxes, width, skeleton)
    gains = packed[:, 2 * width :].astype(jnp.float32).reshape(boxes, pad // 2, 1, skeleton)
    transfers = jnp.concatenate([comp_transfer, exp_transfer], axis=0)
    for number, stride in enumerate(strides):
        halves = state.reshape(boxes // (2 * stride), 2, stride, width, skeleton)
        stacked = jnp.concatenate([halves[:, 0], halves[:, 1]], axis=-1)
        paired = transfers[number].reshape(2, skeleton, 2 * skeleton)
        both = jnp.einsum("hlsk,tjk->htlsj", stacked, paired, preferred_element_type=jnp.float32)
        both = both.reshape(boxes, width, skeleton)
        if number + 1 < len(strides):
            both = both * gains[:, number]
        state = both.astype(jnp.bfloat16)
    return state.reshape(boxes, width, 2, LANES).swapaxes(1, 2).reshape(boxes, 2 * width, LANES)


def plain_decode(packed, decoder):
    boxes, rows, _ = packed.shape
    width = rows // 2
    coeffs = packed.reshape(boxes, 2, width, LANES).swapaxes(1, 2).reshape(boxes * width, 2 * LANES)
    return mm(decoder, coeffs, NT).astype(jnp.bfloat16)


def body(
    sources,
    enc_scale,
    encoder,
    comp_transfer,
    comp_gain,
    exp_transfer,
    exp_gain,
    decoder,
    dec_scale,
):
    col_count, row_count = lax.axis_size("col"), lax.axis_size("row")
    parts = col_count * row_count
    skeleton = encoder.shape[0]
    comp_levels, exp_levels = comp_transfer.shape[0], exp_transfer.shape[0]
    strides = tuple(2**number for number in range(comp_levels))
    strides += tuple(col_count * 2**number for number in range(exp_levels))
    comp_gain, exp_gain = comp_gain[:, 0], exp_gain[:, 0]
    pad = gain_rows(comp_gain, exp_gain)
    last_gain = lax.dynamic_index_in_dim(exp_gain[-1], lax.axis_index("row"), 0, keepdims=False)
    factors = dec_scale[:, None] * last_gain[None, :]
    width = sources.shape[1]
    side = width // 4

    if side % LANES or (width - side) % (8 * parts) or skeleton != 2 * LANES:
        packed = plain_encode(sources, enc_scale, encoder, comp_gain, exp_gain, parts)
        packed = lax.all_to_all(packed, ORDER, 0, 0, tiled=True)
        packed = plain_levels(packed, comp_transfer, exp_transfer, strides, pad)
        packed = lax.all_to_all(packed, ORDER, 0, 0, tiled=True)
        return plain_decode(packed, (decoder.astype(jnp.float32) * factors).astype(jnp.bfloat16))

    sources, encoder = in_hbm(sources), in_hbm(encoder)
    packed = encode(sources, enc_scale, encoder, comp_gain, exp_gain, parts, side)
    packed = lax.all_to_all(packed, ORDER, 0, 0, tiled=True)
    coeffs = side_encode(sources, enc_scale, encoder, side)
    rows = pick(exp_transfer)
    for number in range(comp_levels):
        coeffs = side_level(coeffs, "col", number, comp_transfer, comp_gain)
    packed = levels(packed, comp_transfer, exp_transfer, strides, pad)
    packed = lax.all_to_all(packed, ORDER, 0, 0, tiled=True)
    for number in range(exp_levels - 1):
        coeffs = side_level(coeffs, "row", number, rows[number], exp_gain)
    partner = from_partner(coeffs, "row", exp_levels - 1)
    table = on_chip((decoder.astype(jnp.float32) * factors).astype(jnp.bfloat16))
    field = decode(packed, table, side)
    return side_decode(exp_levels - 1, coeffs, partner, rows[exp_levels - 1], table, field)


def solution(mesh):
    in_specs = (
        P(AXES, None),
        P(AXES),
        P(),
        P(),
        P(None, "row", None, None),
        P(),
        P(None, "col", None, None),
        P(),
        P(AXES),
    )

    def step(*args):
        return jax.shard_map(body, mesh=mesh, in_specs=in_specs, out_specs=P(AXES, None), check_vma=False)(*args)

    return step
```
